256 devices in a mesh: rep: 4 (over y), tp: 64 (over x, z, core).
Axes of the slice: x: 4, y: 4, z: 8, core: 2. Of those that a mesh axis runs over, the one named last changes fastest.
Arguments:
- stream: bfloat16 [1024, 5120], P(('rep', 'tp')), parts along dimension 0, may hold values from -6 to 6
- attn_gain: bfloat16 [5120], replicated, may hold values from 0.5 to 1.5
- query_weight: bfloat16 [5120, 64, 80], P(None, 'tp'), may hold values from -0.078125 to 0.078125
- query_bias_input: bfloat16 [64, 80], P('tp'), may hold values from -2 to 18
- key_value_weight: bfloat16 [5120, 64, 32], P(None, 'tp'), may hold values from -0.078125 to 0.078125
- key_value_bias: bfloat16 [64, 32], P('tp'), may hold values from -2 to 16
- output_weight: bfloat16 [64, 80, 5120], P('tp'), may hold values from -0.078125 to 0.078125
- mlp_gain: bfloat16 [5120], replicated, may hold values from 0.5 to 1.5
- w_gate: bfloat16 [5120, 16384], P(None, 'tp'), may hold values from -0.078125 to 0.078125
- w_up: bfloat16 [5120, 16384], P(None, 'tp'), may hold values from -0.078125 to 0.078125
- w_down: bfloat16 [16384, 5120], P('tp'), may hold values from -0.046875 to 0.046875
- paged_cache_input: bfloat16 [256, 64, 16, 256], P(('rep', 'tp')), parts along dimension 0, may hold values from -6 to 6
- lengths: int32 [8], P('rep'), parts along dimension 0, may hold values from 768 to 3072, as said below
- page_table: int32 [8, 192], P('rep'), parts along dimension 0, may hold values from 0 to 511, as said below
- new_pages: int32 [8, 8], P('rep'), parts along dimension 0, may hold values from 0 to 511, as said below
- mig_from: int32 [32, 8], P('rep'), parts along dimension 0, may hold values from 0 to 63, as said below
- mig_to: int32 [32, 8], P('rep'), parts along dimension 0, may hold values from 0 to 63, as said below
Outputs:
- layer_out: bfloat16 [1024, 5120], P(('rep', 'tp')), parts along dimension 0
- updated_cache: bfloat16 [256, 64, 16, 256], P(('rep', 'tp')), parts along dimension 0
The draws below stay inside these ranges and needn't reach their ends.
There are 4 independent parts, one for each index of `rep`. The reference program is written for one: setup_inputs(seed, part) draws one part's arguments, and reference() takes and returns one part's arrays. A program takes and returns all parts, laid end to end along the dimension named above; an argument that names none is the same for every part. Nothing has to cross between parts.
Inputs may be any that keep to these rules, and one draw needn't show every extreme that they name: `lengths`: one prompt holds exactly 3072 cached tokens. Entries of page_table and new_pages are all distinct; entries past a prompt's length are not read. `new_pages`: distinct from every page_table entry. `mig_from`: 8 distinct slots of owner b that no table names. `mig_to`: 8 distinct slots of owner (b + 1) mod 8, each named by page_table within its prompt's length.
All inputs are finite; a program needn't handle non-finite values.
Results may differ from the reference program's by a relative error of at most 0.0085.
The reference program's roundings to bfloat16 on the way count: a program that leaves them out, or rounds other values in their place, can miss the bound.
Values may be sent and summed in bfloat16 or wider, within the bound.
A program may use at most 128 MiB of HBM per device.

```python
import jax
import jax.numpy as jnp
from jax import lax

MODEL_WIDTH = 5120
QUERY_HEADS = 40
KEY_VALUE_HEADS = 8
HEAD_SIZE = 128
FF = 16384
BATCH_REQUESTS = 2
SPAN = 128
PROMPTS = 2
CMAX = 3072
PAGE_TOKENS = 16
MIG = 8
QUERY_PER_KV = 5
HEAD_OWNERS = 8
OWNER_SLOTS = 64
OWNER_Q_COLUMNS = 80
OWNER_KV_COLUMNS = 32
MAXP = 192
REQUEST_PAGES = 8
NEW_TOKEN_COUNT = 256
N_TP = 64


def page_plan(key):
    base_key = jax.random.fold_in(key, 11)
    sub_keys = jax.random.split(base_key, 3)
    owner_keys = jax.random.split(sub_keys[0], HEAD_OWNERS)
    orders = jax.vmap(lambda each_key: jax.random.permutation(each_key, OWNER_SLOTS))(owner_keys).astype(jnp.int32)
    offsets = (jnp.arange(HEAD_OWNERS, dtype=jnp.int32) * OWNER_SLOTS)[:, None]
    global_ids = orders + offsets
    forced = global_ids[:, MIG:2 * MIG].reshape(-1)
    spare_ids = jax.random.permutation(sub_keys[1], global_ids[:, 2 * MIG:].reshape(-1))
    front_pages = CMAX // 4 // PAGE_TOKENS
    front_count = PROMPTS * front_pages
    count_forced = HEAD_OWNERS * MIG
    head_part = jax.random.permutation(sub_keys[2], jnp.concatenate([forced, spare_ids[:front_count - count_forced]]))
    head_part = head_part.reshape(PROMPTS, front_pages)
    tail_count = PROMPTS * (MAXP - front_pages)
    tail_start = front_count - count_forced
    tail_part = spare_ids[tail_start:tail_start + tail_count].reshape(PROMPTS, MAXP - front_pages)
    page_rows = jnp.concatenate([head_part, tail_part], axis=1).astype(jnp.int32)
    fresh_start = tail_start + tail_count
    fresh_pages = spare_ids[fresh_start:fresh_start + BATCH_REQUESTS * REQUEST_PAGES].reshape(BATCH_REQUESTS, REQUEST_PAGES).astype(jnp.int32)
    sources = orders[:, :MIG]
    targets = jnp.roll(orders[:, MIG:2 * MIG], -1, axis=0)
    return (page_rows, fresh_pages, sources, targets)


def draw_page_table(key, part):
    return page_plan(key)[0]


def draw_new_pages(key, part):
    return page_plan(key)[1]


def draw_mig_from(key, part):
    return page_plan(key)[2]


def draw_mig_to(key, part):
    return page_plan(key)[3]


def draw_lengths(key, part):
    base_key = jax.random.fold_in(key, 23)
    sub_keys = jax.random.split(base_key, 2)
    full_index = jax.random.randint(sub_keys[0], (), 0, PROMPTS)
    others = jax.random.randint(sub_keys[1], (PROMPTS,), CMAX // 4, CMAX + 1)
    return jnp.where(jnp.arange(PROMPTS) == full_index, CMAX, others).astype(jnp.int32)


def draw_query_bias_input(key, part):
    base_key = jax.random.fold_in(key, 31)
    sub_keys = jax.random.split(base_key, 1)
    noise = 0.5 * jax.random.truncated_normal(sub_keys[0], -4.0, 4.0, (N_TP, OWNER_Q_COLUMNS), jnp.float32)
    return noise.astype(jnp.bfloat16)


def draw_key_value_bias(key, part):
    base_key = jax.random.fold_in(key, 37)
    sub_keys = jax.random.split(base_key, 1)
    noise = 0.5 * jax.random.truncated_normal(sub_keys[0], -4.0, 4.0, (N_TP, OWNER_KV_COLUMNS), jnp.float32)
    return noise.astype(jnp.bfloat16)


def steps_of(key, shape, cuts, smallest, largest):
    loudness, own = 1.0, jax.random.fold_in(key, 6)
    for axis_at, shards_of in cuts:
        steps = jnp.exp(jax.random.uniform(jax.random.fold_in(own, axis_at), (shards_of,), jnp.float32, smallest / len(cuts), largest / len(cuts)))
        loudness = loudness * jnp.repeat(steps, shape[axis_at] // shards_of).reshape([-1 if axis == axis_at else 1 for axis in range(len(shape))])
    return loudness


def bell_draw(own_key, extent, scale, reach, pieces=(), kind=jnp.bfloat16):
    gain = steps_of(own_key, extent, pieces, -0.22, 0.18) if pieces else 1.0
    drawn = jax.random.normal(own_key, extent, jnp.float32) * scale * gain
    return jnp.minimum(jnp.maximum(drawn, -reach), reach).astype(kind)


def setup_inputs(seed: int = 0, part: int = 0) -> dict:
    seeds = jax.random.split(jax.random.key(seed), 18)
    own_keys = jax.random.split(jax.random.fold_in(seeds[17], part), 18)
    return {
        "stream": bell_draw(own_keys[0], (NEW_TOKEN_COUNT, MODEL_WIDTH), 1.0, 6.0, ((0, 64),)),
        "attn_gain": jnp.clip(1.0 + 0.1 * jax.random.normal(seeds[1], (MODEL_WIDTH,), jnp.float32), 0.5, 1.5).astype(jnp.bfloat16),
        "query_weight": bell_draw(seeds[2], (MODEL_WIDTH, N_TP, OWNER_Q_COLUMNS), MODEL_WIDTH ** -0.5, 0.078125, ((1, 64),)),
        "query_bias_input": draw_query_bias_input(jax.random.fold_in(seeds[17], 71), part),
        "key_value_weight": bell_draw(seeds[4], (MODEL_WIDTH, N_TP, OWNER_KV_COLUMNS), MODEL_WIDTH ** -0.5, 0.078125, ((1, 64),)),
        "key_value_bias": draw_key_value_bias(jax.random.fold_in(seeds[17], 71), part),
        "output_weight": bell_draw(seeds[6], (N_TP, OWNER_Q_COLUMNS, MODEL_WIDTH), (QUERY_HEADS * HEAD_SIZE) ** -0.5, 0.078125, ((0, 64),)),
        "mlp_gain": jnp.clip(1.0 + 0.1 * jax.random.normal(seeds[7], (MODEL_WIDTH,), jnp.float32), 0.5, 1.5).astype(jnp.bfloat16),
        "w_gate": bell_draw(seeds[8], (MODEL_WIDTH, FF), MODEL_WIDTH ** -0.5, 0.078125, ((1, 64),)),
        "w_up": bell_draw(seeds[9], (MODEL_WIDTH, FF), MODEL_WIDTH ** -0.5, 0.078125, ((1, 64),)),
        "w_down": bell_draw(seeds[10], (FF, MODEL_WIDTH), FF ** -0.5, 0.046875, ((0, 64),)),
        "paged_cache_input": bell_draw(own_keys[11], (N_TP, OWNER_SLOTS, PAGE_TOKENS, 2 * HEAD_SIZE), 1.0, 6.0, ((0, 64),)),
        "lengths": draw_lengths(jax.random.fold_in(jax.random.fold_in(seeds[17], part), 71), part),
        "page_table": draw_page_table(jax.random.fold_in(jax.random.fold_in(seeds[17], part), 71), part),
        "new_pages": draw_new_pages(jax.random.fold_in(jax.random.fold_in(seeds[17], part), 71), part),
        "mig_from": draw_mig_from(jax.random.fold_in(jax.random.fold_in(seeds[17], part), 71), part),
        "mig_to": draw_mig_to(jax.random.fold_in(jax.random.fold_in(seeds[17], part), 71), part),
    }


EPSILON = 1e-06
ROPE_BASE = 1000000.0
NEG_LARGE = -1e+30

def rms_scale(values, gain_vec):
    widened = values.astype(jnp.float32)
    spread = lax.optimization_barrier(jnp.mean(widened * widened, axis=-1, keepdims=True))
    return (widened * lax.rsqrt(spread + EPSILON) * gain_vec.astype(jnp.float32)).astype(jnp.bfloat16)

def rotary(values, positions):
    half_dim = values.shape[-1] // 2
    frequencies = ROPE_BASE ** (-(2.0 * jnp.arange(half_dim, dtype=jnp.float32)) / values.shape[-1])
    angles = positions.astype(jnp.float32)[:, None] * frequencies[None, :]
    cosine = jnp.cos(angles)[:, None, :]
    sine_part = jnp.sin(angles)[:, None, :]
    first_half = values[..., :half_dim]
    second = values[..., half_dim:]
    return jnp.concatenate([first_half * cosine - second * sine_part, second * cosine + first_half * sine_part], axis=-1)

def token_info(lengths):
    token_ids = jnp.arange(NEW_TOKEN_COUNT, dtype=jnp.int32)
    request_of = token_ids // SPAN
    offset_of = token_ids % SPAN
    prompt_of = request_of
    positions = (jnp.take(lengths, prompt_of) + offset_of).astype(jnp.int32)
    return (request_of, offset_of, prompt_of, positions)

def slot_roles(slot_ids, page_table, new_pages):
    old_hit = (page_table[:, :, None] == slot_ids[None, None, :]).astype(jnp.int32)
    old_valid = lax.optimization_barrier(jnp.sum(old_hit, axis=(0, 1))).astype(jnp.int32)
    old_prompt = lax.optimization_barrier(jnp.sum(old_hit * jnp.arange(PROMPTS, dtype=jnp.int32)[:, None, None], axis=(0, 1))).astype(jnp.int32)
    old_page = lax.optimization_barrier(jnp.sum(old_hit * jnp.arange(MAXP, dtype=jnp.int32)[None, :, None], axis=(0, 1))).astype(jnp.int32)
    new_hit = (new_pages[:, :, None] == slot_ids[None, None, :]).astype(jnp.int32)
    new_valid = lax.optimization_barrier(jnp.sum(new_hit, axis=(0, 1))).astype(jnp.int32)
    new_request = lax.optimization_barrier(jnp.sum(new_hit * jnp.arange(BATCH_REQUESTS, dtype=jnp.int32)[:, None, None], axis=(0, 1))).astype(jnp.int32)
    new_page = lax.optimization_barrier(jnp.sum(new_hit * jnp.arange(REQUEST_PAGES, dtype=jnp.int32)[None, :, None], axis=(0, 1))).astype(jnp.int32)
    return (old_valid, old_prompt, old_page, new_valid, new_request, new_page)

def key_allowed(roles, lengths, request_of, offset_of, prompt_of):
    old_valid, old_prompt, old_page, new_valid, new_request, new_page = roles
    within_page = jnp.arange(PAGE_TOKENS, dtype=jnp.int32)
    old_pos = (old_page[:, None] * PAGE_TOKENS + within_page[None, :]).reshape(-1)
    new_pos = (new_page[:, None] * PAGE_TOKENS + within_page[None, :]).reshape(-1)
    old_limit = jnp.repeat(jnp.take(lengths, old_prompt).astype(jnp.int32), PAGE_TOKENS)
    old_ok = (jnp.repeat(old_valid, PAGE_TOKENS) == 1)[None, :] & (jnp.repeat(old_prompt, PAGE_TOKENS)[None, :] == prompt_of[:, None]) & (old_pos < old_limit)[None, :]
    new_ok = (jnp.repeat(new_valid, PAGE_TOKENS) == 1)[None, :] & (jnp.repeat(new_request, PAGE_TOKENS)[None, :] == request_of[:, None]) & (new_pos[None, :] <= offset_of[:, None])
    return old_ok | new_ok

def take_slots(one_block, slot_list):
    return one_block[:, slot_list]

def put_slots(one_block, slot_list, page_data):
    return one_block.at[:, slot_list].set(page_data)

def reference(stream, attn_gain, query_weight, query_bias_input, key_value_weight, key_value_bias, output_weight, mlp_gain, w_gate, w_up, w_down, paged_cache_input, lengths, page_table, new_pages, mig_from, mig_to):
    query_weight_matrix = query_weight.reshape(MODEL_WIDTH, HEAD_OWNERS, KEY_VALUE_HEADS, OWNER_Q_COLUMNS).transpose(0, 2, 1, 3).reshape(MODEL_WIDTH, QUERY_HEADS * HEAD_SIZE)
    query_bias_rows = query_bias_input.reshape(HEAD_OWNERS, KEY_VALUE_HEADS, OWNER_Q_COLUMNS).transpose(1, 0, 2).reshape(QUERY_HEADS * HEAD_SIZE)
    key_value_matrix = key_value_weight.reshape(MODEL_WIDTH, HEAD_OWNERS, KEY_VALUE_HEADS, OWNER_KV_COLUMNS).transpose(0, 2, 1, 3).reshape(MODEL_WIDTH, KEY_VALUE_HEADS * 2 * HEAD_SIZE)
    key_value_bias_rows = key_value_bias.reshape(HEAD_OWNERS, KEY_VALUE_HEADS, OWNER_KV_COLUMNS).transpose(1, 0, 2).reshape(KEY_VALUE_HEADS * 2 * HEAD_SIZE)
    output_matrix = output_weight.reshape(HEAD_OWNERS, KEY_VALUE_HEADS, OWNER_Q_COLUMNS, MODEL_WIDTH).transpose(1, 0, 2, 3).reshape(QUERY_HEADS * HEAD_SIZE, MODEL_WIDTH)
    normed = rms_scale(stream, attn_gain)
    queries = (jnp.dot(normed, query_weight_matrix, preferred_element_type=jnp.float32) + query_bias_rows.astype(jnp.float32)).astype(jnp.bfloat16)
    key_value_rows = (jnp.dot(normed, key_value_matrix, preferred_element_type=jnp.float32) + key_value_bias_rows.astype(jnp.float32)).astype(jnp.bfloat16)
    key_value_rows = key_value_rows.reshape(NEW_TOKEN_COUNT, KEY_VALUE_HEADS, 2 * HEAD_SIZE)
    request_of, offset_of, prompt_of, positions = token_info(lengths)
    rotated_queries = rotary(queries.reshape(NEW_TOKEN_COUNT, QUERY_HEADS, HEAD_SIZE).astype(jnp.float32), positions).astype(jnp.bfloat16)
    keys_rot = rotary(key_value_rows[:, :, :HEAD_SIZE].astype(jnp.float32), positions).astype(jnp.bfloat16)
    appended_rows = jnp.concatenate([keys_rot, key_value_rows[:, :, HEAD_SIZE:]], axis=-1)
    block_list = paged_cache_input.reshape(HEAD_OWNERS, KEY_VALUE_HEADS, OWNER_SLOTS, PAGE_TOKENS, 2 * HEAD_SIZE)
    moved_pages = jax.vmap(take_slots)(block_list, mig_from)
    received_pages = jnp.roll(moved_pages, 1, axis=0)
    landing = jnp.roll(mig_to, 1, axis=0)
    block_list = jax.vmap(put_slots)(block_list, landing, received_pages)
    flattened_cache = block_list.transpose(1, 0, 2, 3, 4).reshape(KEY_VALUE_HEADS, HEAD_OWNERS * OWNER_SLOTS, PAGE_TOKENS, 2 * HEAD_SIZE)
    written_cache = appended_rows.reshape(BATCH_REQUESTS * REQUEST_PAGES, PAGE_TOKENS, KEY_VALUE_HEADS, 2 * HEAD_SIZE).transpose(2, 0, 1, 3)
    flattened_cache = flattened_cache.at[:, new_pages.reshape(-1)].set(written_cache)
    updated_cache = flattened_cache.reshape(KEY_VALUE_HEADS, HEAD_OWNERS, OWNER_SLOTS, PAGE_TOKENS, 2 * HEAD_SIZE).transpose(1, 0, 2, 3, 4).reshape(N_TP, OWNER_SLOTS, PAGE_TOKENS, 2 * HEAD_SIZE)

    def owner_mask(owned_ids):
        return key_allowed(slot_roles(owned_ids, page_table, new_pages), lengths, request_of, offset_of, prompt_of)
    slot_ids = jnp.arange(HEAD_OWNERS * OWNER_SLOTS, dtype=jnp.int32).reshape(HEAD_OWNERS, OWNER_SLOTS)
    masks = jax.vmap(owner_mask)(slot_ids)
    grouped_query = rotated_queries.reshape(NEW_TOKEN_COUNT, KEY_VALUE_HEADS, QUERY_PER_KV, HEAD_SIZE).transpose(1, 0, 2, 3)
    grouped_key_value = flattened_cache.reshape(KEY_VALUE_HEADS, HEAD_OWNERS, OWNER_SLOTS * PAGE_TOKENS, 2 * HEAD_SIZE)

    def attend_group(inputs):
        group_q, group_kv = inputs

        def owner_part(owner_kv, mask_rows):
            scores = jnp.einsum('tqd,kd->qtk', group_q.astype(jnp.float32), owner_kv[:, :HEAD_SIZE].astype(jnp.float32)) * HEAD_SIZE ** (-0.5)
            live_mask = mask_rows[None]
            part_max = lax.optimization_barrier(jnp.max(jnp.where(live_mask, scores, NEG_LARGE), axis=-1))
            weights = jnp.where(live_mask, jnp.exp(scores - part_max[..., None]), 0.0)
            part_sum = lax.optimization_barrier(jnp.sum(weights, axis=-1))
            prob_bf = weights.astype(jnp.bfloat16)
            part_out = jnp.einsum('qtk,kd->tqd', prob_bf.astype(jnp.float32), owner_kv[:, HEAD_SIZE:].astype(jnp.float32))
            return (part_max, part_sum, part_out)
        maxima, totals, outputs = jax.vmap(owner_part)(group_kv, masks)
        top_max = lax.optimization_barrier(jnp.max(maxima, axis=0))
        factor = jnp.exp(maxima - top_max[None])
        numerator = lax.optimization_barrier(jnp.sum(factor.transpose(0, 2, 1)[..., None] * outputs, axis=0))
        denominator = lax.optimization_barrier(jnp.sum(factor * totals, axis=0)).T
        return (numerator / denominator[..., None]).astype(jnp.bfloat16)
    attended = lax.map(attend_group, (grouped_query, grouped_key_value))
    attended = attended.transpose(1, 0, 2, 3).reshape(NEW_TOKEN_COUNT, QUERY_HEADS * HEAD_SIZE)
    mixed_rows = (stream.astype(jnp.float32) + jnp.dot(attended, output_matrix, preferred_element_type=jnp.float32)).astype(jnp.bfloat16)
    normed_mlp = rms_scale(mixed_rows, mlp_gain)
    gate_acts = jnp.dot(normed_mlp, w_gate, preferred_element_type=jnp.float32)
    up_acts = jnp.dot(normed_mlp, w_up, preferred_element_type=jnp.float32)
    hidden = (jax.nn.silu(gate_acts) * up_acts).astype(jnp.bfloat16)
    layer_out = (mixed_rows.astype(jnp.float32) + jnp.dot(hidden, w_down, preferred_element_type=jnp.float32)).astype(jnp.bfloat16)
    return (layer_out, updated_cache)
```

```python
import jax
import jax.numpy as jnp
from jax import lax
from jax.experimental import pallas as pl
from jax.experimental.pallas import tpu as pltpu
from jax.sharding import PartitionSpec as P

KEY_VALUE_HEADS = 8
HEAD_SIZE = 128
BATCH_REQUESTS = 2
SPAN = 128
PROMPTS = 2
PAGE_TOKENS = 16
QUERY_PER_KV = 5
MAXP = 192
REQUEST_PAGES = 8
NEW_TOKEN_COUNT = 256
NX, NZ = 4, 8
ROWS = 4
CLASS_ROWS = 128
WIDTH = 5120
HALF = WIDTH // 2
MESH = pl.DeviceIdType.MESH
BF16, F32 = jnp.bfloat16, jnp.float32


EPSILON = 1e-06
ROPE_BASE = 1000000.0
NEG_LARGE = -1e30


def from_partner(value, axis, distance):
    mask = 2**distance
    pairs = [(source, source ^ mask) for source in range(lax.axis_size(axis))]
    return lax.ppermute(value, axis, pairs)


def passed_along(value, axis, steps):
    count = lax.axis_size(axis)
    pairs = [(source, (source + steps) % count) for source in range(count)]
    return lax.ppermute(value, axis, pairs)


def rotary(values, positions):
    half_dim = values.shape[-1] // 2
    frequencies = ROPE_BASE ** (-(2.0 * jnp.arange(half_dim, dtype=jnp.float32)) / values.shape[-1])
    angles = positions.astype(jnp.float32)[:, None] * frequencies[None, :]
    cosine = jnp.cos(angles)[:, None, :]
    sine_part = jnp.sin(angles)[:, None, :]
    first_half = values[..., :half_dim]
    second = values[..., half_dim:]
    return jnp.concatenate(
        [first_half * cosine - second * sine_part, second * cosine + first_half * sine_part],
        axis=-1,
    )


def token_info(lengths):
    token_ids = token_order()
    request_of = token_ids // SPAN
    offset_of = token_ids % SPAN
    positions = jnp.take(lengths, request_of) + offset_of
    return (request_of, offset_of, request_of, positions)


def slot_roles(slot_ids, page_table, new_pages):
    old_hit = (page_table[:, :, None] == slot_ids[None, None, :]).astype(jnp.int32)
    old_valid = jnp.sum(old_hit, axis=(0, 1))
    old_prompt = jnp.sum(old_hit * jnp.arange(PROMPTS, dtype=jnp.int32)[:, None, None], axis=(0, 1))
    old_page = jnp.sum(old_hit * jnp.arange(MAXP, dtype=jnp.int32)[None, :, None], axis=(0, 1))
    new_hit = (new_pages[:, :, None] == slot_ids[None, None, :]).astype(jnp.int32)
    new_valid = jnp.sum(new_hit, axis=(0, 1))
    new_request = jnp.sum(
        new_hit * jnp.arange(BATCH_REQUESTS, dtype=jnp.int32)[:, None, None], axis=(0, 1)
    )
    new_page = jnp.sum(
        new_hit * jnp.arange(REQUEST_PAGES, dtype=jnp.int32)[None, :, None], axis=(0, 1)
    )
    return (old_valid, old_prompt, old_page, new_valid, new_request, new_page)


def key_allowed(roles, lengths, request_of, offset_of, prompt_of):
    old_valid, old_prompt, old_page, new_valid, new_request, new_page = roles
    within_page = jnp.arange(PAGE_TOKENS, dtype=jnp.int32)
    old_pos = (old_page[:, None] * PAGE_TOKENS + within_page[None, :]).reshape(-1)
    new_pos = (new_page[:, None] * PAGE_TOKENS + within_page[None, :]).reshape(-1)
    old_limit = jnp.repeat(jnp.take(lengths, old_prompt), PAGE_TOKENS)
    old_ok = (
        (jnp.repeat(old_valid, PAGE_TOKENS) == 1)[None, :]
        & (jnp.repeat(old_prompt, PAGE_TOKENS)[None, :] == prompt_of[:, None])
        & (old_pos < old_limit)[None, :]
    )
    new_ok = (
        (jnp.repeat(new_valid, PAGE_TOKENS) == 1)[None, :]
        & (jnp.repeat(new_request, PAGE_TOKENS)[None, :] == request_of[:, None])
        & (new_pos[None, :] <= offset_of[:, None])
    )
    return old_ok | new_ok


class Place:
    def __init__(self):
        me = lax.axis_index("tp")
        self.x, self.z, self.c = me // 16, (me // 2) % NZ, me % 2

    def at(self, dx=0, dz=0, flip=False):
        x, z = (self.x + dx + NX) % NX, (self.z + dz + NZ) % NZ
        c = 1 - self.c if flip else self.c
        return {"tp": x * 16 + z * 2 + c}

    def around(self):
        return (
            [self.at(dx=d) for d in range(1, NX)]
            + [self.at(dz=d) for d in range(1, NZ)]
            + [self.at(flip=True)]
        )


def remote(src, dst, send_sem, recv_sem, device):
    return pltpu.make_async_remote_copy(
        src_ref=src,
        dst_ref=dst,
        send_sem=send_sem,
        recv_sem=recv_sem,
        device_id=device,
        device_id_type=MESH,
    )


def greet(place):
    barrier = pltpu.get_barrier_semaphore()
    peers = place.around()
    for peer in peers:
        pl.semaphore_signal(barrier, inc=1, device_id=peer, device_id_type=MESH)
    return lambda: pl.semaphore_wait(barrier, len(peers))


def rows_at(index, size):
    return pl.ds(pl.multiple_of(index * size, size), size)


def cols_at(half):
    return pl.ds(half * HALF, HALF)


GATHER_SCRATCH = [
    pltpu.VMEM((NZ, ROWS, WIDTH), BF16),
    pltpu.VMEM((32, WIDTH), F32),
    pltpu.VMEM((2, CLASS_ROWS, WIDTH), BF16),
    pltpu.SemaphoreType.DMA((24,)),
    pltpu.SemaphoreType.DMA((24,)),
    pltpu.SemaphoreType.DMA((2,)),
]


def gather_class(place, block, pieces, tile, gathered, send, recv, pair, along, cls):
    first, second = ("x", "z") if along == "x" else ("z", "x")
    n1, n2 = (NX, NZ) if along == "x" else (NZ, NX)
    i1, i2 = (place.x, place.z) if along == "x" else (place.z, place.x)

    def shift(axis, d):
        return place.at(dx=d) if axis == "x" else place.at(dz=d)

    pending = []
    pieces[i1] = block
    for d in range(1, n1):
        copy = remote(pieces.at[i1], pieces.at[i1], send.at[d - 1], recv.at[d - 1], shift(first, d))
        copy.start()
        pending.append(copy)
    for d in range(1, n1):
        source = (i1 - d + n1) % n1
        remote(
            pieces.at[source], pieces.at[source], send.at[d - 1], recv.at[d - 1], shift(first, d)
        ).wait_recv()
    height = n1 * ROWS
    for j in range(n1):
        tile[j * ROWS : (j + 1) * ROWS, :] = pieces[j].astype(F32)
    gathered[cls, rows_at(i2, height), :] = tile[0:height, :].astype(BF16)

    partner = place.at(flip=True)

    def to_partner(owner, half):
        part = gathered.at[cls, rows_at(owner, height), cols_at(half)]
        remote(part, part, pair.at[0], pair.at[1], partner).start()

    steps = n2 // 2
    for s in range(steps):
        for half in range(2):
            for side, sign in ((0, 1), (1, -1)):
                owner = (i2 - sign * s + n2) % n2
                part = gathered.at[cls, rows_at(owner, height), cols_at(half)]
                slot = 7 + side * 8 + s * 2 + half
                if s >= 1:
                    before = slot - 2
                    remote(
                        part, part, send.at[before], recv.at[before], shift(second, sign)
                    ).wait_recv()
                if s < steps - 1 or half == side:
                    copy = remote(part, part, send.at[slot], recv.at[slot], shift(second, sign))
                    copy.start()
                    pending.append(copy)
                if s >= 1 or side == 0:
                    to_partner(owner, half)
    far = (i2 + steps) % n2
    for side, sign in ((0, 1), (1, -1)):
        part = gathered.at[cls, rows_at(far, height), cols_at(side)]
        slot = 7 + side * 8 + (steps - 1) * 2 + side
        remote(part, part, send.at[slot], recv.at[slot], shift(second, sign)).wait_recv()
        to_partner(far, side)
    for copy in pending:
        copy.wait_send()


def gather_rows(place, block, scratch):
    pieces, tile, gathered, send, recv, pair = scratch

    @pl.when(place.c == 0)
    def _():
        gather_class(place, block, pieces, tile, gathered, send, recv, pair, "x", 0)

    @pl.when(place.c == 1)
    def _():
        gather_class(place, block, pieces, tile, gathered, send, recv, pair, "z", 1)


def gather_pair_wait(place, scratch):
    gathered, pair = scratch[2], scratch[5]
    remote(
        gathered.at[place.c], gathered.at[1 - place.c], pair.at[0], pair.at[1], place.at(flip=True)
    ).wait()


SCATTER_SCRATCH = [
    pltpu.VMEM((CLASS_ROWS, WIDTH), BF16),
    pltpu.VMEM((CLASS_ROWS, WIDTH), BF16),
    pltpu.VMEM((CLASS_ROWS, WIDTH), F32),
    pltpu.VMEM((8, 32, HALF), BF16),
    pltpu.VMEM((8, 32, HALF), BF16),
    pltpu.VMEM((32, WIDTH), F32),
    pltpu.VMEM((NZ, ROWS, WIDTH), BF16),
    pltpu.VMEM((NZ, ROWS, WIDTH), BF16),
    pltpu.VMEM((NZ, ROWS, WIDTH), F32),
    pltpu.VMEM((ROWS, WIDTH), F32),
    pltpu.SemaphoreType.DMA((24,)),
    pltpu.SemaphoreType.DMA((24,)),
    pltpu.SemaphoreType.DMA((2,)),
]


def scatter_class(place, scratch, along):
    _, swapped, own, outgoing, incoming, tile, leaving, arriving, parts, result, send, recv, _ = (
        scratch
    )
    n1, n2 = (NZ, NX) if along == "z" else (NX, NZ)
    i1, i2 = (place.z, place.x) if along == "z" else (place.x, place.z)
    first, second = ("z", "x") if along == "z" else ("x", "z")
    height = n2 * ROWS

    def shift(axis, d):
        return place.at(dx=d) if axis == "x" else place.at(dz=d)

    def slot_of(ref, slot):
        if height == 32:
            return ref.at[slot]
        return ref.at[slot // 2, pl.ds((slot % 2) * 16, 16)]

    def mine(owner, half):
        rows, cols = rows_at(owner, height), cols_at(half)
        return own[rows, cols] + swapped[rows, cols].astype(F32)

    steps = n1 // 2
    pending = []

    def hop(slot, sign):
        return remote(
            slot_of(outgoing, slot),
            slot_of(incoming, slot),
            send.at[slot],
            recv.at[slot],
            shift(first, sign),
        )

    for s in range(steps):
        for half in range(2):
            for side, sign in ((0, 1), (1, -1)):
                begin = 0 if half == side else 1
                if s < begin:
                    continue
                owner = (i1 + sign * (steps - s) + 2 * n1) % n1
                slot = side * steps * 2 + s * 2 + half
                value = mine(owner, half)
                if s > begin:
                    hop(slot - 2, sign).wait_recv()
                    value = value + slot_of(incoming, slot - 2)[...].astype(F32)
                slot_of(outgoing, slot)[...] = value.astype(BF16)
                copy = hop(slot, sign)
                copy.start()
                pending.append(copy)
    for half in range(2):
        value = mine(i1, half)
        for side, sign in ((0, 1), (1, -1)):
            slot = side * steps * 2 + (steps - 1) * 2 + half
            hop(slot, sign).wait_recv()
            value = value + slot_of(incoming, slot)[...].astype(F32)
        tile[0:height, cols_at(half)] = value

    for j in range(n2):
        part = tile[j * ROWS : (j + 1) * ROWS, :]
        parts[j] = part
        leaving[j] = part.astype(BF16)

    def last(d):
        return remote(
            leaving.at[(i2 + d) % n2],
            arriving.at[d],
            send.at[16 + d],
            recv.at[16 + d],
            shift(second, d),
        )

    for d in range(1, n2):
        copy = last(d)
        copy.start()
        pending.append(copy)
    total = parts[i2]
    for d in range(1, n2):
        last(d).wait_recv()
        total = total + arriving[d].astype(F32)
    result[...] = total
    for copy in pending:
        copy.wait_send()


def scatter_sums(place, partial, scratch):
    handed, swapped, own = scratch[:3]
    pair = scratch[12]
    other = 1 - place.c
    chunk = 1280

    @pl.loop(0, WIDTH // chunk)
    def _(k):
        cols = pl.ds(pl.multiple_of(k * chunk, chunk), chunk)
        handed[:, cols] = partial(other, cols).astype(BF16)
        remote(
            handed.at[:, cols], swapped.at[:, cols], pair.at[0], pair.at[1], place.at(flip=True)
        ).start()

    @pl.loop(0, WIDTH // chunk)
    def _(k):
        cols = pl.ds(pl.multiple_of(k * chunk, chunk), chunk)
        own[:, cols] = partial(place.c, cols)

    remote(handed, swapped, pair.at[0], pair.at[1], place.at(flip=True)).wait()

    @pl.when(place.c == 0)
    def _():
        scatter_class(place, scratch, "z")

    @pl.when(place.c == 1)
    def _():
        scatter_class(place, scratch, "x")

    return scratch[9][...]


def rms_block(values, gain_ref):
    spread = jnp.mean(values * values, axis=-1, keepdims=True)
    return (values * lax.rsqrt(spread + EPSILON) * gain_ref[...].astype(F32)).astype(BF16)


def entry_kernel(stream, gain, weight, bias, projected, weight_buf, weight_sem, *gather):
    place = Place()
    ready = greet(place)
    load = pltpu.make_async_copy(weight, weight_buf, weight_sem)
    load.start()
    block = rms_block(stream[...].astype(F32), gain)
    ready()
    gather_rows(place, block, gather)
    load.wait()

    def project(cls):
        sums = jnp.dot(gather[2][cls], weight_buf[...], preferred_element_type=F32)
        projected[cls] = (sums + bias[...].astype(F32)).astype(BF16)

    project(place.c)
    gather_pair_wait(place, gather)
    project(1 - place.c)


def exit_kernel(
    attended, stream, gain, out_w, gate_w, up_w, down_w, layer_out,
    out_buf, gate_buf, up_buf, down_buf, hidden, load_sems, *comm
):
    first, gather, second = comm[:13], comm[13:19], comm[19:]
    place = Place()
    ready = greet(place)
    loads = [
        pltpu.make_async_copy(src, dst, load_sems.at[k])
        for k, (src, dst) in enumerate(
            ((out_w, out_buf), (gate_w, gate_buf), (up_w, up_buf), (down_w, down_buf))
        )
    ]
    for load in loads:
        load.start()
    loads[0].wait()
    ready()

    def out_term(cls, cols):
        return jnp.dot(attended[cls], out_buf[:, cols], preferred_element_type=F32)

    summed = scatter_sums(place, out_term, first)
    mixed = (stream[...].astype(F32) + summed).astype(BF16)
    block = rms_block(mixed.astype(F32), gain)
    gather_rows(place, block, gather)
    loads[1].wait()
    loads[2].wait()

    def hide(cls):
        rows = gather[2][cls]
        gate = jnp.dot(rows, gate_buf[...], preferred_element_type=F32)
        up = jnp.dot(rows, up_buf[...], preferred_element_type=F32)
        hidden[cls] = (gate / (1.0 + jnp.exp(-gate)) * up).astype(BF16)

    hide(place.c)
    gather_pair_wait(place, gather)
    hide(1 - place.c)
    loads[3].wait()

    def down_term(cls, cols):
        return jnp.dot(hidden[cls], down_buf[:, cols], preferred_element_type=F32)

    summed = scatter_sums(place, down_term, second)
    layer_out[...] = (mixed.astype(F32) + summed).astype(BF16)


VM = pl.BlockSpec(memory_space=pltpu.VMEM)
ANY = pl.BlockSpec(memory_space=pl.ANY)


def entry(stream, gain, weight, bias):
    columns = weight.shape[1]
    return pl.pallas_call(
        entry_kernel,
        out_shape=jax.ShapeDtypeStruct((2, CLASS_ROWS, columns), BF16),
        in_specs=[VM, VM, ANY, VM],
        out_specs=VM,
        scratch_shapes=[pltpu.VMEM(weight.shape, BF16), pltpu.SemaphoreType.DMA] + GATHER_SCRATCH,
        compiler_params=pltpu.CompilerParams(collective_id=0, has_side_effects=True),
        name="entry",
    )(stream, gain[None], weight, bias[None])


def leave(attended, stream, gain, out_w, gate_w, up_w, down_w):
    buffers = [pltpu.VMEM(w.shape, BF16) for w in (out_w, gate_w, up_w, down_w)]
    return pl.pallas_call(
        exit_kernel,
        out_shape=jax.ShapeDtypeStruct((ROWS, WIDTH), BF16),
        in_specs=[VM, VM, VM, ANY, ANY, ANY, ANY],
        out_specs=VM,
        scratch_shapes=buffers
        + [pltpu.VMEM((2, CLASS_ROWS, gate_w.shape[1]), BF16), pltpu.SemaphoreType.DMA((4,))]
        + SCATTER_SCRATCH
        + GATHER_SCRATCH
        + SCATTER_SCRATCH,
        compiler_params=pltpu.CompilerParams(
            collective_id=1, has_side_effects=True, vmem_limit_bytes=60 * 2**20
        ),
        name="leave",
    )(attended, stream, gain[None], out_w, gate_w, up_w, down_w)


def token_order():
    row = jnp.arange(CLASS_ROWS, dtype=jnp.int32)
    z, x, r = row // 16, row // ROWS % NX, row % ROWS
    zero = (x * 16 + z * 2) * ROWS + r
    x, z = row // 32, row // ROWS % NZ
    one = (x * 16 + z * 2 + 1) * ROWS + r
    return jnp.concatenate([zero, one])


def row_of_token(token):
    device, r = token // ROWS, token % ROWS
    x, z, c = device // 16, device // 2 % NZ, device % 2
    return jnp.where(c == 0, z * 16 + x * ROWS, CLASS_ROWS + x * 32 + z * ROWS) + r


def per_device(
    stream,
    attn_gain,
    query_weight,
    query_bias_input,
    key_value_weight,
    key_value_bias,
    output_weight,
    mlp_gain,
    w_gate,
    w_up,
    w_down,
    paged_cache_input,
    lengths,
    page_table,
    new_pages,
    mig_from,
    mig_to,
):
    device_total = lax.axis_size("tp")
    owner_total = device_total // KEY_VALUE_HEADS
    level_count = owner_total.bit_length() - 1
    group_flag = KEY_VALUE_HEADS.bit_length() - 1
    token_position = lax.axis_index("tp")
    owner_index = token_position // KEY_VALUE_HEADS
    tok_rows = stream.shape[0]
    total_rows = tok_rows * device_total
    query_cols = query_weight.shape[2]
    proj_weight = jnp.concatenate([query_weight[:, 0, :], key_value_weight[:, 0, :]], axis=1)
    proj_bias = jnp.concatenate([query_bias_input[0], key_value_bias[0]])
    projected = entry(stream, attn_gain, proj_weight, proj_bias).reshape(total_rows, -1)
    gathered = projected
    for each_level in range(level_count):
        partner = from_partner(gathered, "tp", group_flag + each_level)
        upper_side = owner_index >> each_level & 1 == 1
        gathered = jnp.where(
            upper_side,
            jnp.concatenate([partner, gathered], axis=1),
            jnp.concatenate([gathered, partner], axis=1),
        )
    pieces = gathered.reshape(total_rows, owner_total, -1)
    queries = pieces[:, :, :query_cols].reshape(total_rows, QUERY_PER_KV, HEAD_SIZE)
    key_value_rows = pieces[:, :, query_cols:].reshape(total_rows, 2 * HEAD_SIZE)
    request_of, offset_of, prompt_of, positions = token_info(lengths)
    rotated_queries = rotary(queries.astype(jnp.float32), positions).astype(jnp.bfloat16)
    keys_rot = rotary(key_value_rows[:, None, :HEAD_SIZE].astype(jnp.float32), positions)[
        :, 0
    ].astype(jnp.bfloat16)
    appended_rows = jnp.concatenate([keys_rot, key_value_rows[:, HEAD_SIZE:]], axis=1)
    local_cache = paged_cache_input[0]
    slot_count = local_cache.shape[0]
    departing_pages = local_cache[
        lax.dynamic_index_in_dim(mig_from, owner_index, 0, keepdims=False)
    ]
    received_pages = passed_along(departing_pages, "tp", KEY_VALUE_HEADS)
    sender = (owner_index + owner_total - 1) % owner_total
    landing = lax.dynamic_index_in_dim(mig_to, sender, 0, keepdims=False)
    local_cache = local_cache.at[landing].set(received_pages)
    slot_ids = owner_index * slot_count + jnp.arange(slot_count, dtype=jnp.int32)
    roles = slot_roles(slot_ids, page_table, new_pages)
    new_valid, new_request, new_page = (roles[3], roles[4], roles[5])
    source_rows = (new_request * SPAN + new_page * PAGE_TOKENS)[:, None] + jnp.arange(
        PAGE_TOKENS, dtype=jnp.int32
    )[None, :]
    fresh_pages = appended_rows[row_of_token(source_rows)]
    local_cache = jnp.where((new_valid == 1)[:, None, None], fresh_pages, local_cache)
    updated_cache = local_cache[None]
    allowed = key_allowed(roles, lengths, request_of, offset_of, prompt_of)
    flat_keys = local_cache.reshape(slot_count * PAGE_TOKENS, 2 * HEAD_SIZE)
    scores = jnp.einsum(
        "tqd,kd->qtk", rotated_queries, flat_keys[:, :HEAD_SIZE], preferred_element_type=jnp.float32
    ) * HEAD_SIZE ** (-0.5)
    live_mask = allowed[None]
    part_max = jnp.max(jnp.where(live_mask, scores, NEG_LARGE), axis=-1)
    weights = jnp.where(live_mask, jnp.exp(scores - part_max[..., None]), 0.0)
    part_sum = jnp.sum(weights, axis=-1).T
    part_max = part_max.T
    prob_bf = weights.astype(jnp.bfloat16)
    part_out = jnp.einsum(
        "qtk,kd->tqd", prob_bf, flat_keys[:, HEAD_SIZE:], preferred_element_type=jnp.float32
    )
    merged = part_out.reshape(total_rows, QUERY_PER_KV * HEAD_SIZE)
    for each_level in range(level_count):
        other_out, other_max, other_sum = from_partner(
            (merged, part_max, part_sum), "tp", group_flag + each_level
        )
        both_max = jnp.maximum(part_max, other_max)
        mine_weight = jnp.exp(part_max - both_max)
        other_weight = jnp.exp(other_max - both_max)
        merged = (
            merged.reshape(total_rows, QUERY_PER_KV, HEAD_SIZE) * mine_weight[..., None]
            + other_out.reshape(total_rows, QUERY_PER_KV, HEAD_SIZE) * other_weight[..., None]
        ).reshape(total_rows, QUERY_PER_KV * HEAD_SIZE)
        part_sum = mine_weight * part_sum + other_weight * other_sum
        part_max = both_max
    normalized = (
        merged.reshape(total_rows, QUERY_PER_KV, HEAD_SIZE) / part_sum[..., None]
    ).reshape(total_rows, QUERY_PER_KV * HEAD_SIZE)
    attn_piece = lax.dynamic_slice_in_dim(
        normalized, owner_index * query_cols, query_cols, 1
    ).astype(jnp.bfloat16)
    layer_out = leave(
        attn_piece.reshape(2, CLASS_ROWS, query_cols),
        stream, mlp_gain, output_weight[0], w_gate, w_up, w_down,
    )
    return (layer_out, updated_cache)


def solution(mesh):
    placed = (
        P(("rep", "tp"), None),
        P(),
        P(None, "tp", None),
        P("tp", None),
        P(None, "tp", None),
        P("tp", None),
        P("tp", None, None),
        P(),
        P(None, "tp"),
        P(None, "tp"),
        P("tp", None),
        P(("rep", "tp"), None, None, None),
        P("rep"),
        P("rep", None),
        P("rep", None),
        P("rep", None),
        P("rep", None),
    )
    return jax.shard_map(
        per_device,
        mesh=mesh,
        in_specs=placed,
        out_specs=(P(("rep", "tp"), None), P(("rep", "tp"), None, None, None)),
        check_vma=False,
    )
```

```python
import math

import jax
import jax.numpy as jnp
from jax import lax
from jax.experimental import pallas as pl
from jax.experimental.pallas import tpu as pltpu
from jax.sharding import PartitionSpec as P

KEY_VALUE_HEADS = 8
HEAD_SIZE = 128
SPAN = 128
PAGE_TOKENS = 16
QUERY_PER_KV = 5
REQUEST_PAGES = 8
TOKENS = 256
OWNERS = 8
SLOTS = 64
KEYS = SLOTS * PAGE_TOKENS
MIGRATED = 8
Q_COLS, KV_COLS = 80, 32
PACK = 96
NX, NZ = 4, 8
ROWS = 4
CLASS_ROWS = 128
WIDTH = 5120
HALF = WIDTH // 2
MESH = pl.DeviceIdType.MESH
BF16, F32 = jnp.bfloat16, jnp.float32


EPSILON = 1e-06
ROPE_BASE = 1000000.0
NEG_LARGE = -1e30
LOG_BASE = math.log(ROPE_BASE)


class Place:
    def __init__(self):
        me = lax.axis_index("tp")
        self.x, self.z, self.c = me // 16, (me // 2) % NZ, me % 2

    def at(self, dx=0, dz=0, flip=False):
        x, z = (self.x + dx + NX) % NX, (self.z + dz + NZ) % NZ
        c = 1 - self.c if flip else self.c
        return {"tp": x * 16 + z * 2 + c}

    def owner(self):
        return self.x * 2 + self.z // 4

    def around(self):
        return (
            [self.at(dx=d) for d in range(1, NX)]
            + [self.at(dz=d) for d in range(1, NZ)]
            + [self.at(flip=True)]
        )


def remote(src, dst, send_sem, recv_sem, device):
    return pltpu.make_async_remote_copy(
        src_ref=src,
        dst_ref=dst,
        send_sem=send_sem,
        recv_sem=recv_sem,
        device_id=device,
        device_id_type=MESH,
    )


def greet(place, more=()):
    barrier = pltpu.get_barrier_semaphore()
    peers = place.around() + list(more)
    for peer in peers:
        pl.semaphore_signal(barrier, inc=1, device_id=peer, device_id_type=MESH)
    return lambda: pl.semaphore_wait(barrier, len(peers))


def rows_at(index, size):
    return pl.ds(pl.multiple_of(index * size, size), size)


def cols_at(half):
    return pl.ds(half * HALF, HALF)


GATHER_SCRATCH = [
    pltpu.VMEM((NZ, ROWS, WIDTH), BF16),
    pltpu.VMEM((32, WIDTH), F32),
    pltpu.VMEM((2, CLASS_ROWS, WIDTH), BF16),
    pltpu.SemaphoreType.DMA((24,)),
    pltpu.SemaphoreType.DMA((24,)),
    pltpu.SemaphoreType.DMA((2,)),
]


def gather_class(place, block, pieces, tile, gathered, send, recv, pair, along, cls, extra):
    first, second = ("x", "z") if along == "x" else ("z", "x")
    n1, n2 = (NX, NZ) if along == "x" else (NZ, NX)
    i1, i2 = (place.x, place.z) if along == "x" else (place.z, place.x)

    def shift(axis, d):
        return place.at(dx=d) if axis == "x" else place.at(dz=d)

    pending = []
    pieces[i1] = block
    for d in range(1, n1):
        copy = remote(pieces.at[i1], pieces.at[i1], send.at[d - 1], recv.at[d - 1], shift(first, d))
        copy.start()
        pending.append(copy)
    extra()
    for d in range(1, n1):
        source = (i1 - d + n1) % n1
        remote(
            pieces.at[source], pieces.at[source], send.at[d - 1], recv.at[d - 1], shift(first, d)
        ).wait_recv()
    height = n1 * ROWS
    for j in range(n1):
        tile[j * ROWS : (j + 1) * ROWS, :] = pieces[j].astype(F32)
    gathered[cls, rows_at(i2, height), :] = tile[0:height, :].astype(BF16)

    partner = place.at(flip=True)

    def to_partner(owner, half):
        part = gathered.at[cls, rows_at(owner, height), cols_at(half)]
        remote(part, part, pair.at[0], pair.at[1], partner).start()

    steps = n2 // 2
    for s in range(steps):
        for half in range(2):
            for side, sign in ((0, 1), (1, -1)):
                owner = (i2 - sign * s + n2) % n2
                part = gathered.at[cls, rows_at(owner, height), cols_at(half)]
                slot = 7 + side * 8 + s * 2 + half
                if s >= 1:
                    before = slot - 2
                    remote(
                        part, part, send.at[before], recv.at[before], shift(second, sign)
                    ).wait_recv()
                if s < steps - 1 or half == side:
                    copy = remote(part, part, send.at[slot], recv.at[slot], shift(second, sign))
                    copy.start()
                    pending.append(copy)
                if s >= 1 or side == 0:
                    to_partner(owner, half)
    far = (i2 + steps) % n2
    for side, sign in ((0, 1), (1, -1)):
        part = gathered.at[cls, rows_at(far, height), cols_at(side)]
        slot = 7 + side * 8 + (steps - 1) * 2 + side
        remote(part, part, send.at[slot], recv.at[slot], shift(second, sign)).wait_recv()
        to_partner(far, side)
    for copy in pending:
        copy.wait_send()


def gather_rows(place, block, scratch, extra=lambda: None):
    pieces, tile, gathered, send, recv, pair = scratch

    @pl.when(place.c == 0)
    def _():
        gather_class(place, block, pieces, tile, gathered, send, recv, pair, "x", 0, extra)

    @pl.when(place.c == 1)
    def _():
        gather_class(place, block, pieces, tile, gathered, send, recv, pair, "z", 1, extra)


def gather_pair_wait(place, scratch):
    gathered, pair = scratch[2], scratch[5]
    remote(
        gathered.at[place.c], gathered.at[1 - place.c], pair.at[0], pair.at[1], place.at(flip=True)
    ).wait()


SCATTER_SCRATCH = [
    pltpu.VMEM((CLASS_ROWS, WIDTH), BF16),
    pltpu.VMEM((CLASS_ROWS, WIDTH), BF16),
    pltpu.VMEM((CLASS_ROWS, WIDTH), F32),
    pltpu.VMEM((8, 32, HALF), BF16),
    pltpu.VMEM((8, 32, HALF), BF16),
    pltpu.VMEM((32, WIDTH), F32),
    pltpu.VMEM((NZ, ROWS, WIDTH), BF16),
    pltpu.VMEM((NZ, ROWS, WIDTH), BF16),
    pltpu.VMEM((NZ, ROWS, WIDTH), F32),
    pltpu.VMEM((ROWS, WIDTH), F32),
    pltpu.SemaphoreType.DMA((24,)),
    pltpu.SemaphoreType.DMA((24,)),
    pltpu.SemaphoreType.DMA((2,)),
]


def scatter_class(place, scratch, along):
    _, swapped, own, outgoing, incoming, tile, leaving, arriving, parts, result, send, recv, _ = (
        scratch
    )
    n1, n2 = (NZ, NX) if along == "z" else (NX, NZ)
    i1, i2 = (place.z, place.x) if along == "z" else (place.x, place.z)
    first, second = ("z", "x") if along == "z" else ("x", "z")
    height = n2 * ROWS

    def shift(axis, d):
        return place.at(dx=d) if axis == "x" else place.at(dz=d)

    def slot_of(ref, slot):
        if height == 32:
            return ref.at[slot]
        return ref.at[slot // 2, pl.ds((slot % 2) * 16, 16)]

    def mine(owner, half):
        rows, cols = rows_at(owner, height), cols_at(half)
        return own[rows, cols] + swapped[rows, cols].astype(F32)

    steps = n1 // 2
    pending = []

    def hop(slot, sign):
        return remote(
            slot_of(outgoing, slot),
            slot_of(incoming, slot),
            send.at[slot],
            recv.at[slot],
            shift(first, sign),
        )

    for s in range(steps):
        for half in range(2):
            for side, sign in ((0, 1), (1, -1)):
                begin = 0 if half == side else 1
                if s < begin:
                    continue
                owner = (i1 + sign * (steps - s) + 2 * n1) % n1
                slot = side * steps * 2 + s * 2 + half
                value = mine(owner, half)
                if s > begin:
                    hop(slot - 2, sign).wait_recv()
                    value = value + slot_of(incoming, slot - 2)[...].astype(F32)
                slot_of(outgoing, slot)[...] = value.astype(BF16)
                copy = hop(slot, sign)
                copy.start()
                pending.append(copy)
    for half in range(2):
        value = mine(i1, half)
        for side, sign in ((0, 1), (1, -1)):
            slot = side * steps * 2 + (steps - 1) * 2 + half
            hop(slot, sign).wait_recv()
            value = value + slot_of(incoming, slot)[...].astype(F32)
        tile[0:height, cols_at(half)] = value

    for j in range(n2):
        part = tile[j * ROWS : (j + 1) * ROWS, :]
        parts[j] = part
        leaving[j] = part.astype(BF16)

    def last(d):
        return remote(
            leaving.at[(i2 + d) % n2],
            arriving.at[d],
            send.at[16 + d],
            recv.at[16 + d],
            shift(second, d),
        )

    for d in range(1, n2):
        copy = last(d)
        copy.start()
        pending.append(copy)
    total = parts[i2]
    for d in range(1, n2):
        last(d).wait_recv()
        total = total + arriving[d].astype(F32)
    result[...] = total
    for copy in pending:
        copy.wait_send()


def scatter_sums(place, partial, scratch):
    handed, swapped, own = scratch[:3]
    pair = scratch[12]
    other = 1 - place.c
    chunk = 1280

    @pl.loop(0, WIDTH // chunk)
    def _(k):
        cols = pl.ds(pl.multiple_of(k * chunk, chunk), chunk)
        handed[:, cols] = partial(other, cols).astype(BF16)
        remote(
            handed.at[:, cols], swapped.at[:, cols], pair.at[0], pair.at[1], place.at(flip=True)
        ).start()

    @pl.loop(0, WIDTH // chunk)
    def _(k):
        cols = pl.ds(pl.multiple_of(k * chunk, chunk), chunk)
        own[:, cols] = partial(place.c, cols)

    remote(handed, swapped, pair.at[0], pair.at[1], place.at(flip=True)).wait()

    @pl.when(place.c == 0)
    def _():
        scatter_class(place, scratch, "z")

    @pl.when(place.c == 1)
    def _():
        scatter_class(place, scratch, "x")

    return scratch[9][...]


def rms_block(values, gain_ref):
    spread = jnp.mean(values * values, axis=-1, keepdims=True)
    lines = gain_ref[...].astype(F32)
    gain = jnp.concatenate([lines[k : k + 1] for k in range(WIDTH // 128)], axis=1)
    return (values * lax.rsqrt(spread + EPSILON) * gain).astype(BF16)


def across(a, b):
    return lax.dot_general(a, b, (((1,), (1,)), ((), ())), preferred_element_type=F32)


def entry_kernel(
    stream, gain, query_w, kv_w, query_b, kv_b, cache, mig_from, pieces, landed,
    weight_buf, cache_buf, leaving, load_sems, page_sems, send, recv, *gather
):
    place = Place()
    owner = place.owner()
    side = place.z // 4
    ready = greet(place, (place.at(dx=1, dz=4), place.at(dx=-1, dz=4)))
    loads = [
        pltpu.make_async_copy(query_w, weight_buf.at[0:Q_COLS], load_sems.at[0]),
        pltpu.make_async_copy(kv_w, weight_buf.at[Q_COLS : Q_COLS + KV_COLS], load_sems.at[1]),
        pltpu.make_async_copy(cache, cache_buf, load_sems.at[2]),
    ]
    for load in loads:
        load.start()
    weight_buf[Q_COLS + KV_COLS :, :] = jnp.zeros((128 - Q_COLS - KV_COLS, WIDTH), BF16)
    block = rms_block(stream[...].astype(F32), gain)
    ready()
    pages = remote(leaving, landed, page_sems.at[0], page_sems.at[1], place.at(dx=side, dz=4))

    def send_pages():
        loads[2].wait()
        for j in range(MIGRATED):
            leaving[j] = cache_buf[mig_from[owner, j]]
        pages.start()

    gather_rows(place, block, gather, send_pages)
    loads[0].wait()
    loads[1].wait()
    bias = jnp.concatenate(
        [
            query_b[...].astype(F32),
            kv_b[...].astype(F32),
            jnp.zeros((1, 128 - Q_COLS - KV_COLS), F32),
        ],
        axis=1,
    )
    pending = []

    def part(who, cls, slot, device):
        ref = pieces.at[who, cls]
        return remote(ref, ref, send.at[slot], recv.at[slot], device)

    def project(cls, base):
        pieces[owner, cls] = (across(gather[2][cls], weight_buf[...]) + bias).astype(BF16)
        for k, device in enumerate([place.at(dz=4)] + [place.at(dx=d) for d in range(1, NX)]):
            copy = part(owner, cls, base + k, device)
            copy.start()
            pending.append(copy)

    project(place.c, 0)
    gather_pair_wait(place, gather)
    project(1 - place.c, 4)
    opposite = place.x * 2 + 1 - side
    for k, cls in enumerate((place.c, 1 - place.c)):
        part(opposite, cls, 4 * k, place.at(dz=4)).wait_recv()
        for d in range(1, NX):
            copy = part(opposite, cls, 8 + 3 * k + d - 1, place.at(dx=d))
            copy.start()
            pending.append(copy)
    for d in range(1, NX):
        x = (place.x - d + NX) % NX
        for k, cls in enumerate((place.c, 1 - place.c)):
            part(x * 2 + side, cls, 4 * k + d, place.at(dx=d)).wait_recv()
            part(x * 2 + 1 - side, cls, 8 + 3 * k + d - 1, place.at(dx=d)).wait_recv()
    for copy in pending:
        copy.wait_send()
    pages.wait()


def row_facts(shape, axis):
    row = lax.broadcasted_iota(jnp.int32, shape, axis)
    inner = row % CLASS_ROWS
    r = row % ROWS
    first = row < CLASS_ROWS
    x = jnp.where(first, inner // ROWS % NX, inner // 32)
    z = jnp.where(first, inner // 16, inner // ROWS % NZ)
    c = jnp.where(first, 0, 1)
    token = (x * 16 + z * 2 + c) * ROWS + r
    return token // SPAN, token % SPAN


def spread_of(values, lane, step, count):
    total = jnp.zeros(lane.shape, jnp.int32)
    for j in range(count):
        total = jnp.where(lane // step == j, values(j), total)
    return total


def new_queries(pieces, lengths, queries):
    apart = lax.broadcasted_iota(jnp.int32, (128, 128), 1) - lax.broadcasted_iota(
        jnp.int32, (128, 128), 0
    )
    source = lax.broadcasted_iota(jnp.int32, (128, 128), 0)

    def block(start, first, columns, width):
        total = None
        for who in range(start // width, (start + 127) // width + 1):
            pick = (apart == who * width - start - first) & (source >= first) & (source < first + width)
            pick = pick.astype(F32).astype(BF16)
            term = jnp.dot(
                pieces[who].reshape(TOKENS, 128), pick, preferred_element_type=F32
            )
            total = term if total is None else total + term
        return total

    request, offset = row_facts((TOKENS, 128), 0)
    lane = lax.broadcasted_iota(jnp.int32, (TOKENS, 128), 1)
    rate = jnp.exp((lane % 64).astype(F32) * (-2.0 / HEAD_SIZE * LOG_BASE))
    position = (jnp.where(request == 0, lengths[0], lengths[1]) + offset).astype(F32)
    angle = position * rate
    cosine = jnp.cos(angle)
    sine = jnp.where(lane < 64, -1.0, 1.0) * jnp.sin(angle)

    def rotate(values):
        return (values * cosine + pltpu.roll(values, 64, 1) * sine).astype(BF16)

    for h in range(QUERY_PER_KV):
        queries[h] = rotate(block(h * HEAD_SIZE, 0, 0, Q_COLS))
    keys = rotate(block(0, Q_COLS, 0, KV_COLS))
    values = block(HEAD_SIZE, Q_COLS, 0, KV_COLS).astype(BF16)
    return jnp.concatenate([keys, values], axis=1)


def split_rows(rows):
    out = []
    for row in rows:
        high = row.astype(BF16).astype(F32)
        middle = (row - high).astype(BF16).astype(F32)
        out += [high, middle, row - high - middle]
    return out


def stack_rows(rows, count):
    at = lax.broadcasted_iota(jnp.int32, (count, TOKENS), 0)
    total = jnp.zeros((count, TOKENS), F32)
    for k, row in enumerate(rows):
        total = jnp.where(at == k, row, total)
    return total


def attend_kernel(
    pieces, landed, cache, lengths, page_table, new_pages_v, new_pages, mig_to, packed, updated,
    queries, joined,
):
    owner = Place().owner()
    new_rows = new_queries(pieces, lengths, queries)

    slot = lax.broadcasted_iota(jnp.int32, (SLOTS, page_table.shape[1]), 0) + owner * SLOTS
    entry_at = lax.broadcasted_iota(jnp.int32, slot.shape, 1) + 1
    new_slot, new_at = slot[:, :REQUEST_PAGES], entry_at[:, :REQUEST_PAGES]

    def found(table, r, ids, at):
        hit = jnp.where(table[r : r + 1, :] == ids, at, 0).astype(F32)
        return jnp.sum(hit, axis=1, keepdims=True)

    facts = [
        found(page_table, 0, slot, entry_at),
        found(page_table, 1, slot, entry_at),
        found(new_pages_v, 0, new_slot, new_at),
        found(new_pages_v, 1, new_slot, new_at),
    ]
    sender = (owner + OWNERS - 1) % OWNERS
    own_slot = lax.broadcasted_iota(jnp.int32, (SLOTS, 1), 0)
    landing = jnp.zeros((SLOTS, 1), F32)
    for j in range(MIGRATED):
        landing = jnp.where(own_slot == mig_to[sender, j], 1.0, landing)
    facts.append(landing)
    lane = lax.broadcasted_iota(jnp.int32, (SLOTS, 128), 1)
    table = jnp.zeros((SLOTS, 128), F32)
    for k, fact in enumerate(facts):
        table = jnp.where(lane == k, fact, table)
    key = lax.broadcasted_iota(jnp.int32, (KEYS, SLOTS), 0)
    belongs = key // PAGE_TOKENS == lax.broadcasted_iota(jnp.int32, (KEYS, SLOTS), 1)
    by_key = jnp.dot(
        belongs.astype(F32).astype(BF16), table.astype(BF16), preferred_element_type=F32
    )
    within = (lax.broadcasted_iota(jnp.int32, (KEYS, 1), 0) % PAGE_TOKENS).astype(F32)

    def least(r):
        old, new = by_key[:, r : r + 1], by_key[:, 2 + r : 3 + r]
        old_ok = (old > 0.5) & ((old - 1.0) * PAGE_TOKENS + within < lengths[r].astype(F32))
        new_first = jnp.where(new > 0.5, (new - 1.0) * PAGE_TOKENS + within, 1e9)
        return jnp.where(old_ok, 0.0, new_first)

    request, offset = row_facts((1, TOKENS), 1)
    needed = jnp.where(request == 0, least(0), least(1))
    bias = jnp.where(offset.astype(F32) >= needed, 0.0, NEG_LARGE)

    total = MIGRATED * PAGE_TOKENS + TOKENS
    lane = lax.broadcasted_iota(jnp.int32, (1, MIGRATED * PAGE_TOKENS), 1)
    migrated_to = (
        spread_of(lambda j: mig_to[sender, j], lane, PAGE_TOKENS, MIGRATED) * PAGE_TOKENS
        + lane % PAGE_TOKENS
    )
    page = request * REQUEST_PAGES + offset // PAGE_TOKENS
    written_to = spread_of(
        lambda j: new_pages[j // REQUEST_PAGES, j % REQUEST_PAGES], page, 1, 2 * REQUEST_PAGES
    )
    written_to = jnp.where(
        written_to // SLOTS == owner, written_to % SLOTS * PAGE_TOKENS + offset % PAGE_TOKENS, -1
    )
    target = jnp.concatenate([migrated_to, written_to], axis=1)
    pick = lax.broadcasted_iota(jnp.int32, (KEYS, total), 0) == target
    arrived = jnp.concatenate(
        [landed[...].reshape(MIGRATED * PAGE_TOKENS, 2 * HEAD_SIZE), new_rows], axis=0
    )
    fresh = jnp.dot(pick.astype(F32).astype(BF16), arrived, preferred_element_type=F32)
    changed = by_key[:, 2:3] + by_key[:, 3:4] + by_key[:, 4:5] > 0.5
    rows = jnp.where(
        changed, fresh, cache[...].reshape(KEYS, 2 * HEAD_SIZE).astype(F32)
    )
    kept = rows.astype(BF16)
    updated[...] = kept.reshape(updated.shape)
    keys = kept[:, :HEAD_SIZE]
    values = rows[:, HEAD_SIZE:].T.astype(BF16)
    tops, sums = [], []
    for h in range(QUERY_PER_KV):
        scores = across(keys, queries[h]) * HEAD_SIZE ** (-0.5) + bias
        top = jnp.max(scores, axis=0, keepdims=True)
        weights = jnp.exp(scores - top)
        tops.append(top)
        sums.append(jnp.sum(weights, axis=0, keepdims=True))
        joined[h * HEAD_SIZE : (h + 1) * HEAD_SIZE, :] = jnp.dot(
            values, weights.astype(BF16), preferred_element_type=F32
        ).astype(BF16)
    for who in range(OWNERS):
        one = who * Q_COLS // HEAD_SIZE
        two = min(one + 1, QUERY_PER_KV - 1)
        packed[who, 0:Q_COLS, :] = joined[who * Q_COLS : (who + 1) * Q_COLS, :]
        packed[who, Q_COLS:, :] = stack_rows(
            split_rows([tops[one], tops[two], sums[one], sums[two]]), PACK - Q_COLS
        ).astype(BF16)


def unpack(ref_value):
    value = ref_value.astype(F32)
    rows = [value[Q_COLS + k : Q_COLS + k + 1] for k in range(12)]
    facts = [rows[3 * k] + rows[3 * k + 1] + rows[3 * k + 2] for k in range(4)]
    return value[:Q_COLS], facts


def merge(parts, who):
    head_end = (who * Q_COLS // HEAD_SIZE + 1) * HEAD_SIZE - who * Q_COLS
    in_first = lax.broadcasted_iota(jnp.int32, (Q_COLS, TOKENS), 0) < head_end
    tops = [parts[0][1][0], parts[0][1][1]]
    for _, facts in parts[1:]:
        tops = [jnp.maximum(tops[k], facts[k]) for k in range(2)]
    total, sums = 0.0, [0.0, 0.0]
    for values, facts in parts:
        scale = [jnp.exp(facts[k] - tops[k]) for k in range(2)]
        sums = [sums[k] + scale[k] * facts[2 + k] for k in range(2)]
        total = total + values * jnp.where(in_first, scale[0], scale[1])
    return total, tops + sums, in_first


def merge_owners(place, packed, near, far, leaving, send, recv):
    side = place.z // 4
    pending = []
    for d in range(1, NX):
        x = (place.x + d) % NX
        copy = remote(
            packed.at[pl.ds(x * 2, 2)], near.at[d - 1], send.at[d], recv.at[d], place.at(dx=d)
        )
        copy.start()
        pending.append(copy)
    for copy in pending:
        copy.wait_recv()

    def gathered(which):
        who = place.x * 2 + which
        parts = [unpack(packed[who])] + [unpack(near[d, which]) for d in range(NX - 1)]
        return merge(parts, who)

    total, facts, _ = gathered(1 - side)
    leaving[0:Q_COLS, :] = total.astype(BF16)
    leaving[Q_COLS:, :] = stack_rows(split_rows(facts), PACK - Q_COLS).astype(BF16)
    copy = remote(leaving, far, send.at[0], recv.at[0], place.at(dz=4))
    copy.start()
    pending.append(copy)
    total, facts, _ = gathered(side)
    copy.wait_recv()
    total, facts, in_first = merge([(total, facts), unpack(far[...])], place.owner())
    for copy in pending:
        copy.wait_send()
    return total / jnp.where(in_first, facts[2], facts[3])


MERGE_SCRATCH = [
    pltpu.VMEM((NX - 1, 2, PACK, TOKENS), BF16),
    pltpu.VMEM((PACK, TOKENS), BF16),
    pltpu.VMEM((PACK, TOKENS), BF16),
    pltpu.SemaphoreType.DMA((NX,)),
    pltpu.SemaphoreType.DMA((NX,)),
]


def exit_kernel(
    packed, stream, gain, out_w, gate_w, up_w, down_w, layer_out,
    out_buf, gate_buf, up_buf, down_buf, hidden, attended, load_sems, *comm
):
    joining, first, gather, second = comm[:5], comm[5:18], comm[18:24], comm[24:]
    place = Place()
    ready = greet(place)
    loads = [
        pltpu.make_async_copy(src, dst, load_sems.at[k])
        for k, (src, dst) in enumerate(
            (
                (out_w, out_buf.at[0:Q_COLS]),
                (gate_w, gate_buf),
                (up_w, up_buf),
                (down_w, down_buf),
            )
        )
    ]
    for load in loads:
        load.start()
    out_buf[Q_COLS:, :] = jnp.zeros((128 - Q_COLS, WIDTH), BF16)
    ready()
    columns = merge_owners(place, packed, *joining)
    columns = jnp.concatenate([columns, jnp.zeros((128 - Q_COLS, TOKENS), F32)], axis=0)
    attended[...] = columns.T.astype(BF16).reshape(attended.shape)
    loads[0].wait()

    def out_term(cls, cols):
        return jnp.dot(attended[cls], out_buf[:, cols], preferred_element_type=F32)

    summed = scatter_sums(place, out_term, first)
    mixed = (stream[...].astype(F32) + summed).astype(BF16)
    block = rms_block(mixed.astype(F32), gain)
    gather_rows(place, block, gather)
    loads[1].wait()
    loads[2].wait()

    def hide(cls):
        rows = gather[2][cls]
        gate = jnp.dot(rows, gate_buf[...], preferred_element_type=F32)
        up = jnp.dot(rows, up_buf[...], preferred_element_type=F32)
        hidden[cls] = (gate / (1.0 + jnp.exp(-gate)) * up).astype(BF16)

    hide(place.c)
    gather_pair_wait(place, gather)
    hide(1 - place.c)
    loads[3].wait()

    def down_term(cls, cols):
        return jnp.dot(hidden[cls], down_buf[:, cols], preferred_element_type=F32)

    summed = scatter_sums(place, down_term, second)
    layer_out[...] = (mixed.astype(F32) + summed).astype(BF16)


VM = pl.BlockSpec(memory_space=pltpu.VMEM)
SM = pl.BlockSpec(memory_space=pltpu.SMEM)
ANY = pl.BlockSpec(memory_space=pl.ANY)
VMEM_BYTES = 60 * 2**20


def entry(stream, gain, query_w, kv_w, query_b, kv_b, cache, mig_from):
    page = (PAGE_TOKENS, 2 * HEAD_SIZE)
    return pl.pallas_call(
        entry_kernel,
        out_shape=(
            jax.ShapeDtypeStruct((OWNERS, 2, CLASS_ROWS, 128), BF16),
            jax.ShapeDtypeStruct((MIGRATED,) + page, BF16),
        ),
        in_specs=[VM, VM, ANY, ANY, VM, VM, ANY, SM],
        out_specs=(VM, VM),
        scratch_shapes=[
            pltpu.VMEM((128, WIDTH), BF16),
            pltpu.VMEM((SLOTS,) + page, BF16),
            pltpu.VMEM((MIGRATED,) + page, BF16),
            pltpu.SemaphoreType.DMA((3,)),
            pltpu.SemaphoreType.DMA((2,)),
            pltpu.SemaphoreType.DMA((14,)),
            pltpu.SemaphoreType.DMA((14,)),
        ]
        + GATHER_SCRATCH,
        compiler_params=pltpu.CompilerParams(
            collective_id=0, has_side_effects=True, vmem_limit_bytes=VMEM_BYTES
        ),
        name="entry",
    )(stream, gain, query_w, kv_w, query_b, kv_b, cache, mig_from)


def attend(pieces, landed, cache, lengths, page_table, new_pages, mig_to):
    return pl.pallas_call(
        attend_kernel,
        out_shape=(
            jax.ShapeDtypeStruct((OWNERS, PACK, TOKENS), BF16),
            jax.ShapeDtypeStruct((1,) + cache.shape, BF16),
        ),
        in_specs=[VM, VM, VM, SM, VM, VM, SM, SM],
        out_specs=(VM, VM),
        scratch_shapes=[
            pltpu.VMEM((QUERY_PER_KV, TOKENS, HEAD_SIZE), BF16),
            pltpu.VMEM((QUERY_PER_KV * HEAD_SIZE, TOKENS), BF16),
        ],
        compiler_params=pltpu.CompilerParams(vmem_limit_bytes=VMEM_BYTES),
        name="attend",
    )(pieces, landed, cache, lengths, page_table, new_pages, new_pages, mig_to)


def leave(packed, stream, gain, out_w, gate_w, up_w, down_w):
    buffers = [
        pltpu.VMEM(shape, BF16)
        for shape in ((128, WIDTH), gate_w.shape, up_w.shape, down_w.shape)
    ]
    return pl.pallas_call(
        exit_kernel,
        out_shape=jax.ShapeDtypeStruct((ROWS, WIDTH), BF16),
        in_specs=[VM, VM, VM, ANY, ANY, ANY, ANY],
        out_specs=VM,
        scratch_shapes=buffers
        + [
            pltpu.VMEM((2, CLASS_ROWS, gate_w.shape[1]), BF16),
            pltpu.VMEM((2, CLASS_ROWS, 128), BF16),
            pltpu.SemaphoreType.DMA((4,)),
        ]
        + MERGE_SCRATCH
        + SCATTER_SCRATCH
        + GATHER_SCRATCH
        + SCATTER_SCRATCH,
        compiler_params=pltpu.CompilerParams(
            collective_id=1, has_side_effects=True, vmem_limit_bytes=VMEM_BYTES
        ),
        name="leave",
    )(packed, stream, gain, out_w, gate_w, up_w, down_w)


def per_device(
    stream,
    attn_gain,
    query_weight,
    query_bias_input,
    key_value_weight,
    key_value_bias,
    output_weight,
    mlp_gain,
    w_gate,
    w_up,
    w_down,
    paged_cache_input,
    lengths,
    page_table,
    new_pages,
    mig_from,
    mig_to,
):
    lines = (WIDTH // 128, 128)
    cache = paged_cache_input[0]
    pieces, landed = entry(
        stream,
        attn_gain.reshape(lines),
        query_weight[:, 0, :].T,
        key_value_weight[:, 0, :].T,
        query_bias_input,
        key_value_bias,
        cache,
        mig_from,
    )
    packed, updated_cache = attend(pieces, landed, cache, lengths, page_table, new_pages, mig_to)
    layer_out = leave(
        packed, stream, mlp_gain.reshape(lines), output_weight[0], w_gate, w_up, w_down
    )
    return (layer_out, updated_cache)


def solution(mesh):
    placed = (
        P(("rep", "tp"), None),
        P(),
        P(None, "tp", None),
        P("tp", None),
        P(None, "tp", None),
        P("tp", None),
        P("tp", None, None),
        P(),
        P(None, "tp"),
        P(None, "tp"),
        P("tp", None),
        P(("rep", "tp"), None, None, None),
        P("rep"),
        P("rep", None),
        P("rep", None),
        P("rep", None),
        P("rep", None),
    )
    return jax.shard_map(
        per_device,
        mesh=mesh,
        in_specs=placed,
        out_specs=(P(("rep", "tp"), None), P(("rep", "tp"), None, None, None)),
        check_vma=False,
    )
```

```python
import math

import jax
import jax.numpy as jnp
from jax import lax
from jax.experimental import pallas as pl
from jax.experimental.pallas import tpu as pltpu
from jax.sharding import PartitionSpec as P

KEY_VALUE_HEADS = 8
HEAD_SIZE = 128
SPAN = 128
PAGE_TOKENS = 16
QUERY_PER_KV = 5
REQUEST_PAGES = 8
TOKENS = 256
OWNERS = 8
SLOTS = 64
KEYS = SLOTS * PAGE_TOKENS
MIGRATED = 8
Q_COLS, KV_COLS = 80, 32
PACK = 96
NX, NZ = 4, 8
ROWS = 4
CLASS_ROWS = 128
WIDTH = 5120
PARTS = 4
PART = WIDTH // PARTS
SEMS = 8 * PARTS + 16
MESH = pl.DeviceIdType.MESH
BF16, F32 = jnp.bfloat16, jnp.float32


EPSILON = 1e-06
ROPE_BASE = 1000000.0
NEG_LARGE = -1e30
LOG_BASE = math.log(ROPE_BASE)


class Place:
    def __init__(self):
        me = lax.axis_index("tp")
        self.x, self.z, self.c = me // 16, (me // 2) % NZ, me % 2

    def at(self, dx=0, dz=0, flip=False):
        x, z = (self.x + dx + NX) % NX, (self.z + dz + NZ) % NZ
        c = 1 - self.c if flip else self.c
        return {"tp": x * 16 + z * 2 + c}

    def owner(self):
        return self.x * 2 + self.z // 4

    def around(self):
        return (
            [self.at(dx=d) for d in range(1, NX)]
            + [self.at(dz=d) for d in range(1, NZ)]
            + [self.at(flip=True)]
        )


def remote(src, dst, send_sem, recv_sem, device):
    return pltpu.make_async_remote_copy(
        src_ref=src,
        dst_ref=dst,
        send_sem=send_sem,
        recv_sem=recv_sem,
        device_id=device,
        device_id_type=MESH,
    )


def greet(place, more=()):
    barrier = pltpu.get_barrier_semaphore()
    peers = place.around() + list(more)
    for peer in peers:
        pl.semaphore_signal(barrier, inc=1, device_id=peer, device_id_type=MESH)
    return lambda: pl.semaphore_wait(barrier, len(peers))


def rows_at(index, size):
    return pl.ds(pl.multiple_of(index * size, size), size)


def cols_at(part):
    return pl.ds(pl.multiple_of(part * PART, PART), PART)


def part_of(k, side):
    return (k + side * PARTS // 2) % PARTS


GATHER_SCRATCH = [
    pltpu.VMEM((NZ, ROWS, WIDTH), BF16),
    pltpu.VMEM((32, WIDTH), F32),
    pltpu.VMEM((2, CLASS_ROWS, WIDTH), BF16),
    pltpu.SemaphoreType.DMA((SEMS,)),
    pltpu.SemaphoreType.DMA((SEMS,)),
    pltpu.SemaphoreType.DMA((2,)),
]


def gather_class(place, block, pieces, tile, gathered, send, recv, pair, along, cls, extra):
    first, second = ("x", "z") if along == "x" else ("z", "x")
    n1, n2 = (NX, NZ) if along == "x" else (NZ, NX)
    i1, i2 = (place.x, place.z) if along == "x" else (place.z, place.x)

    def shift(axis, d):
        return place.at(dx=d) if axis == "x" else place.at(dz=d)

    pending = []
    pieces[i1] = block
    for d in range(1, n1):
        copy = remote(pieces.at[i1], pieces.at[i1], send.at[d - 1], recv.at[d - 1], shift(first, d))
        copy.start()
        pending.append(copy)
    extra()
    for d in range(1, n1):
        source = (i1 - d + n1) % n1
        remote(
            pieces.at[source], pieces.at[source], send.at[d - 1], recv.at[d - 1], shift(first, d)
        ).wait_recv()
    height = n1 * ROWS
    for j in range(n1):
        tile[j * ROWS : (j + 1) * ROWS, :] = pieces[j].astype(F32)
    gathered[cls, rows_at(i2, height), :] = tile[0:height, :].astype(BF16)

    partner = place.at(flip=True)

    def to_partner(ref):
        remote(ref, ref, pair.at[0], pair.at[1], partner).start()

    steps = n2 // 2

    def tile_at(side, s, k):
        owner = (i2 - (1 - 2 * side) * s + n2) % n2
        return gathered.at[cls, rows_at(owner, height), cols_at(part_of(k, side))]

    def hop(ref, side, s, k):
        slot = 7 + (side * steps + s) * PARTS + k
        return remote(ref, ref, send.at[slot], recv.at[slot], shift(second, 1 - 2 * side))

    def landed(side, s, k):
        ref = tile_at(side, s, k)
        hop(ref, side, s - 1, k).wait_recv()
        return ref

    for s in range(steps):
        for k in range(PARTS):
            for side in range(2):
                ref = landed(side, s, k) if s >= 1 else tile_at(side, s, k)
                if s < steps - 1 or k < PARTS // 2:
                    copy = hop(ref, side, s, k)
                    copy.start()
                    pending.append(copy)
                if s >= 1 or side == 0:
                    to_partner(ref)
    for k in range(PARTS // 2):
        for side in range(2):
            to_partner(landed(side, steps, k))
    for copy in pending:
        copy.wait_send()


def gather_rows(place, block, scratch, extra=lambda: None):
    pieces, tile, gathered, send, recv, pair = scratch

    @pl.when(place.c == 0)
    def _():
        gather_class(place, block, pieces, tile, gathered, send, recv, pair, "x", 0, extra)

    @pl.when(place.c == 1)
    def _():
        gather_class(place, block, pieces, tile, gathered, send, recv, pair, "z", 1, extra)


def gather_pair_wait(place, scratch):
    gathered, pair = scratch[2], scratch[5]
    remote(
        gathered.at[place.c], gathered.at[1 - place.c], pair.at[0], pair.at[1], place.at(flip=True)
    ).wait()


SCATTER_SCRATCH = [
    pltpu.VMEM((CLASS_ROWS, WIDTH), BF16),
    pltpu.VMEM((CLASS_ROWS, WIDTH), BF16),
    pltpu.VMEM((CLASS_ROWS, WIDTH), F32),
    pltpu.VMEM((4 * PARTS, 32, PART), BF16),
    pltpu.VMEM((4 * PARTS, 32, PART), BF16),
    pltpu.VMEM((32, WIDTH), F32),
    pltpu.VMEM((NZ, ROWS, WIDTH), BF16),
    pltpu.VMEM((NZ, ROWS, WIDTH), BF16),
    pltpu.VMEM((NZ, ROWS, WIDTH), F32),
    pltpu.VMEM((ROWS, WIDTH), F32),
    pltpu.SemaphoreType.DMA((SEMS,)),
    pltpu.SemaphoreType.DMA((SEMS,)),
    pltpu.SemaphoreType.DMA((2 * PARTS,)),
]


def swap_of(place, scratch):
    handed, swapped, pair = scratch[0], scratch[1], scratch[12]

    def swap(part):
        return remote(
            handed.at[:, cols_at(part)],
            swapped.at[:, cols_at(part)],
            pair.at[part],
            pair.at[PARTS + part],
            place.at(flip=True),
        )

    return swap


def scatter_class(place, scratch, along):
    _, swapped, own, outgoing, incoming, tile, leaving, arriving, parts, result, send, recv, _ = (
        scratch
    )
    swap = swap_of(place, scratch)
    n1, n2 = (NZ, NX) if along == "z" else (NX, NZ)
    i1, i2 = (place.z, place.x) if along == "z" else (place.x, place.z)
    first, second = ("z", "x") if along == "z" else ("x", "z")
    height = n2 * ROWS

    def shift(axis, d):
        return place.at(dx=d) if axis == "x" else place.at(dz=d)

    def slot_of(ref, slot):
        if height == 32:
            return ref.at[slot]
        return ref.at[slot // 2, pl.ds((slot % 2) * 16, 16)]

    def mine(owner, part):
        rows, cols = rows_at(owner, height), cols_at(part)
        return own[rows, cols] + swapped[rows, cols].astype(F32)

    steps = n1 // 2
    pending = []

    def hop(slot, sign):
        return remote(
            slot_of(outgoing, slot),
            slot_of(incoming, slot),
            send.at[slot],
            recv.at[slot],
            shift(first, sign),
        )

    def slot_at(side, s, k):
        return (side * steps + s) * PARTS + k

    early, late = list(range(PARTS // 2)), list(range(PARTS // 2, PARTS))
    for s in range(steps):
        for k in early if s == 0 else late + early:
            for side, sign in ((0, 1), (1, -1)):
                part = part_of(k, side)
                if s == 0:
                    swap(part).wait_recv()
                owner = (i1 + sign * (steps - s) + 2 * n1) % n1
                slot = slot_at(side, s, k)
                value = mine(owner, part)
                if s > (0 if k in early else 1):
                    hop(slot - PARTS, sign).wait_recv()
                    value = value + slot_of(incoming, slot - PARTS)[...].astype(F32)
                slot_of(outgoing, slot)[...] = value.astype(BF16)
                copy = hop(slot, sign)
                copy.start()
                pending.append(copy)
    for part in range(PARTS):
        value = mine(i1, part)
        for side, sign in ((0, 1), (1, -1)):
            slot = slot_at(side, steps - 1, part_of(part, side))
            hop(slot, sign).wait_recv()
            value = value + slot_of(incoming, slot)[...].astype(F32)
        tile[0:height, cols_at(part)] = value

    for j in range(n2):
        part = tile[j * ROWS : (j + 1) * ROWS, :]
        parts[j] = part
        leaving[j] = part.astype(BF16)

    def last(d):
        return remote(
            leaving.at[(i2 + d) % n2],
            arriving.at[d],
            send.at[8 * PARTS + d],
            recv.at[8 * PARTS + d],
            shift(second, d),
        )

    for d in range(1, n2):
        copy = last(d)
        copy.start()
        pending.append(copy)
    total = parts[i2]
    for d in range(1, n2):
        last(d).wait_recv()
        total = total + arriving[d].astype(F32)
    result[...] = total
    for copy in pending:
        copy.wait_send()


def scatter_sums(place, partial, scratch):
    handed, own = scratch[0], scratch[2]
    swap = swap_of(place, scratch)
    other = 1 - place.c

    @pl.loop(0, PARTS // 2)
    def _(k):
        for side in range(2):
            part = k + side * (PARTS // 2)
            cols = cols_at(part)
            handed[:, cols] = partial(other, cols).astype(BF16)
            swap(part).start()

    @pl.loop(0, PARTS // 2)
    def _(k):
        for side in range(2):
            cols = cols_at(k + side * (PARTS // 2))
            own[:, cols] = partial(place.c, cols)

    @pl.when(place.c == 0)
    def _():
        scatter_class(place, scratch, "z")

    @pl.when(place.c == 1)
    def _():
        scatter_class(place, scratch, "x")

    for part in range(PARTS):
        swap(part).wait_send()
    return scratch[9][...]


def rms_block(values, gain_ref):
    spread = jnp.mean(values * values, axis=-1, keepdims=True)
    lines = gain_ref[...].astype(F32)
    gain = jnp.concatenate([lines[k : k + 1] for k in range(WIDTH // 128)], axis=1)
    return (values * lax.rsqrt(spread + EPSILON) * gain).astype(BF16)


def across(a, b):
    return lax.dot_general(a, b, (((1,), (1,)), ((), ())), preferred_element_type=F32)


def entry_kernel(
    stream, gain, query_w, kv_w, query_b, kv_b, cache, mig_from, pieces, landed,
    weight_buf, cache_buf, leaving, load_sems, page_sems, send, recv, *gather
):
    place = Place()
    owner = place.owner()
    side = place.z // 4
    ready = greet(place, (place.at(dx=1, dz=4), place.at(dx=-1, dz=4)))
    loads = [
        pltpu.make_async_copy(query_w, weight_buf.at[0:Q_COLS], load_sems.at[0]),
        pltpu.make_async_copy(kv_w, weight_buf.at[Q_COLS : Q_COLS + KV_COLS], load_sems.at[1]),
        pltpu.make_async_copy(cache, cache_buf, load_sems.at[2]),
    ]
    for load in loads:
        load.start()
    weight_buf[Q_COLS + KV_COLS :, :] = jnp.zeros((128 - Q_COLS - KV_COLS, WIDTH), BF16)
    block = rms_block(stream[...].astype(F32), gain)
    ready()
    pages = remote(leaving, landed, page_sems.at[0], page_sems.at[1], place.at(dx=side, dz=4))

    def send_pages():
        loads[2].wait()
        for j in range(MIGRATED):
            leaving[j] = cache_buf[mig_from[owner, j]]
        pages.start()

    gather_rows(place, block, gather, send_pages)
    loads[0].wait()
    loads[1].wait()
    bias = jnp.concatenate(
        [
            query_b[...].astype(F32),
            kv_b[...].astype(F32),
            jnp.zeros((1, 128 - Q_COLS - KV_COLS), F32),
        ],
        axis=1,
    )
    pending = []

    def part(who, cls, slot, device):
        ref = pieces.at[who, cls]
        return remote(ref, ref, send.at[slot], recv.at[slot], device)

    def project(cls, base):
        pieces[owner, cls] = (across(gather[2][cls], weight_buf[...]) + bias).astype(BF16)
        for k, device in enumerate([place.at(dz=4)] + [place.at(dx=d) for d in range(1, NX)]):
            copy = part(owner, cls, base + k, device)
            copy.start()
            pending.append(copy)

    project(place.c, 0)
    gather_pair_wait(place, gather)
    project(1 - place.c, 4)
    opposite = place.x * 2 + 1 - side
    for k, cls in enumerate((place.c, 1 - place.c)):
        part(opposite, cls, 4 * k, place.at(dz=4)).wait_recv()
        for d in range(1, NX):
            copy = part(opposite, cls, 8 + 3 * k + d - 1, place.at(dx=d))
            copy.start()
            pending.append(copy)
    for d in range(1, NX):
        x = (place.x - d + NX) % NX
        for k, cls in enumerate((place.c, 1 - place.c)):
            part(x * 2 + side, cls, 4 * k + d, place.at(dx=d)).wait_recv()
            part(x * 2 + 1 - side, cls, 8 + 3 * k + d - 1, place.at(dx=d)).wait_recv()
    for copy in pending:
        copy.wait_send()
    pages.wait()


def row_facts(shape, axis):
    row = lax.broadcasted_iota(jnp.int32, shape, axis)
    inner = row % CLASS_ROWS
    r = row % ROWS
    first = row < CLASS_ROWS
    x = jnp.where(first, inner // ROWS % NX, inner // 32)
    z = jnp.where(first, inner // 16, inner // ROWS % NZ)
    c = jnp.where(first, 0, 1)
    token = (x * 16 + z * 2 + c) * ROWS + r
    return token // SPAN, token % SPAN


def spread_of(values, lane, step, count):
    total = jnp.zeros(lane.shape, jnp.int32)
    for j in range(count):
        total = jnp.where(lane // step == j, values(j), total)
    return total


def new_queries(pieces, lengths, queries):
    apart = lax.broadcasted_iota(jnp.int32, (128, 128), 1) - lax.broadcasted_iota(
        jnp.int32, (128, 128), 0
    )
    source = lax.broadcasted_iota(jnp.int32, (128, 128), 0)

    def block(start, first, columns, width):
        total = None
        for who in range(start // width, (start + 127) // width + 1):
            pick = (apart == who * width - start - first) & (source >= first) & (source < first + width)
            pick = pick.astype(F32).astype(BF16)
            term = jnp.dot(
                pieces[who].reshape(TOKENS, 128), pick, preferred_element_type=F32
            )
            total = term if total is None else total + term
        return total

    request, offset = row_facts((TOKENS, 128), 0)
    lane = lax.broadcasted_iota(jnp.int32, (TOKENS, 128), 1)
    rate = jnp.exp((lane % 64).astype(F32) * (-2.0 / HEAD_SIZE * LOG_BASE))
    position = (jnp.where(request == 0, lengths[0], lengths[1]) + offset).astype(F32)
    angle = position * rate
    cosine = jnp.cos(angle)
    sine = jnp.where(lane < 64, -1.0, 1.0) * jnp.sin(angle)

    def rotate(values):
        return (values * cosine + pltpu.roll(values, 64, 1) * sine).astype(BF16)

    for h in range(QUERY_PER_KV):
        queries[h] = rotate(block(h * HEAD_SIZE, 0, 0, Q_COLS))
    keys = rotate(block(0, Q_COLS, 0, KV_COLS))
    values = block(HEAD_SIZE, Q_COLS, 0, KV_COLS).astype(BF16)
    return jnp.concatenate([keys, values], axis=1)


def split_rows(rows):
    out = []
    for row in rows:
        high = row.astype(BF16).astype(F32)
        middle = (row - high).astype(BF16).astype(F32)
        out += [high, middle, row - high - middle]
    return out


def stack_rows(rows, count):
    at = lax.broadcasted_iota(jnp.int32, (count, TOKENS), 0)
    total = jnp.zeros((count, TOKENS), F32)
    for k, row in enumerate(rows):
        total = jnp.where(at == k, row, total)
    return total


def attend_kernel(
    pieces, landed, cache, lengths, page_table, new_pages_v, new_pages, mig_to, packed, updated,
    queries, joined,
):
    owner = Place().owner()
    new_rows = new_queries(pieces, lengths, queries)

    slot = lax.broadcasted_iota(jnp.int32, (SLOTS, page_table.shape[1]), 0) + owner * SLOTS
    entry_at = lax.broadcasted_iota(jnp.int32, slot.shape, 1) + 1
    new_slot, new_at = slot[:, :REQUEST_PAGES], entry_at[:, :REQUEST_PAGES]

    def found(table, r, ids, at):
        hit = jnp.where(table[r : r + 1, :] == ids, at, 0).astype(F32)
        return jnp.sum(hit, axis=1, keepdims=True)

    facts = [
        found(page_table, 0, slot, entry_at),
        found(page_table, 1, slot, entry_at),
        found(new_pages_v, 0, new_slot, new_at),
        found(new_pages_v, 1, new_slot, new_at),
    ]
    sender = (owner + OWNERS - 1) % OWNERS
    own_slot = lax.broadcasted_iota(jnp.int32, (SLOTS, 1), 0)
    landing = jnp.zeros((SLOTS, 1), F32)
    for j in range(MIGRATED):
        landing = jnp.where(own_slot == mig_to[sender, j], 1.0, landing)
    facts.append(landing)
    lane = lax.broadcasted_iota(jnp.int32, (SLOTS, 128), 1)
    table = jnp.zeros((SLOTS, 128), F32)
    for k, fact in enumerate(facts):
        table = jnp.where(lane == k, fact, table)
    key = lax.broadcasted_iota(jnp.int32, (KEYS, SLOTS), 0)
    belongs = key // PAGE_TOKENS == lax.broadcasted_iota(jnp.int32, (KEYS, SLOTS), 1)
    by_key = jnp.dot(
        belongs.astype(F32).astype(BF16), table.astype(BF16), preferred_element_type=F32
    )
    within = (lax.broadcasted_iota(jnp.int32, (KEYS, 1), 0) % PAGE_TOKENS).astype(F32)

    def least(r):
        old, new = by_key[:, r : r + 1], by_key[:, 2 + r : 3 + r]
        old_ok = (old > 0.5) & ((old - 1.0) * PAGE_TOKENS + within < lengths[r].astype(F32))
        new_first = jnp.where(new > 0.5, (new - 1.0) * PAGE_TOKENS + within, 1e9)
        return jnp.where(old_ok, 0.0, new_first)

    request, offset = row_facts((1, TOKENS), 1)
    needed = jnp.where(request == 0, least(0), least(1))
    bias = jnp.where(offset.astype(F32) >= needed, 0.0, NEG_LARGE)

    total = MIGRATED * PAGE_TOKENS + TOKENS
    lane = lax.broadcasted_iota(jnp.int32, (1, MIGRATED * PAGE_TOKENS), 1)
    migrated_to = (
        spread_of(lambda j: mig_to[sender, j], lane, PAGE_TOKENS, MIGRATED) * PAGE_TOKENS
        + lane % PAGE_TOKENS
    )
    page = request * REQUEST_PAGES + offset // PAGE_TOKENS
    written_to = spread_of(
        lambda j: new_pages[j // REQUEST_PAGES, j % REQUEST_PAGES], page, 1, 2 * REQUEST_PAGES
    )
    written_to = jnp.where(
        written_to // SLOTS == owner, written_to % SLOTS * PAGE_TOKENS + offset % PAGE_TOKENS, -1
    )
    target = jnp.concatenate([migrated_to, written_to], axis=1)
    pick = lax.broadcasted_iota(jnp.int32, (KEYS, total), 0) == target
    arrived = jnp.concatenate(
        [landed[...].reshape(MIGRATED * PAGE_TOKENS, 2 * HEAD_SIZE), new_rows], axis=0
    )
    fresh = jnp.dot(pick.astype(F32).astype(BF16), arrived, preferred_element_type=F32)
    changed = by_key[:, 2:3] + by_key[:, 3:4] + by_key[:, 4:5] > 0.5
    rows = jnp.where(
        changed, fresh, cache[...].reshape(KEYS, 2 * HEAD_SIZE).astype(F32)
    )
    kept = rows.astype(BF16)
    updated[...] = kept.reshape(updated.shape)
    keys = kept[:, :HEAD_SIZE]
    values = rows[:, HEAD_SIZE:].T.astype(BF16)
    tops, sums = [], []
    for h in range(QUERY_PER_KV):
        scores = across(keys, queries[h]) * HEAD_SIZE ** (-0.5) + bias
        top = jnp.max(scores, axis=0, keepdims=True)
        weights = jnp.exp(scores - top)
        tops.append(top)
        sums.append(jnp.sum(weights, axis=0, keepdims=True))
        joined[h * HEAD_SIZE : (h + 1) * HEAD_SIZE, :] = jnp.dot(
            values, weights.astype(BF16), preferred_element_type=F32
        ).astype(BF16)
    for who in range(OWNERS):
        one = who * Q_COLS // HEAD_SIZE
        two = min(one + 1, QUERY_PER_KV - 1)
        packed[who, 0:Q_COLS, :] = joined[who * Q_COLS : (who + 1) * Q_COLS, :]
        packed[who, Q_COLS:, :] = stack_rows(
            split_rows([tops[one], tops[two], sums[one], sums[two]]), PACK - Q_COLS
        ).astype(BF16)


def unpack(ref_value):
    value = ref_value.astype(F32)
    rows = [value[Q_COLS + k : Q_COLS + k + 1] for k in range(12)]
    facts = [rows[3 * k] + rows[3 * k + 1] + rows[3 * k + 2] for k in range(4)]
    return value[:Q_COLS], facts


def merge(parts, who):
    head_end = (who * Q_COLS // HEAD_SIZE + 1) * HEAD_SIZE - who * Q_COLS
    in_first = lax.broadcasted_iota(jnp.int32, (Q_COLS, TOKENS), 0) < head_end
    tops = [parts[0][1][0], parts[0][1][1]]
    for _, facts in parts[1:]:
        tops = [jnp.maximum(tops[k], facts[k]) for k in range(2)]
    total, sums = 0.0, [0.0, 0.0]
    for values, facts in parts:
        scale = [jnp.exp(facts[k] - tops[k]) for k in range(2)]
        sums = [sums[k] + scale[k] * facts[2 + k] for k in range(2)]
        total = total + values * jnp.where(in_first, scale[0], scale[1])
    return total, tops + sums, in_first


def merge_owners(place, packed, near, far, leaving, send, recv):
    side = place.z // 4
    pending = []
    for d in range(1, NX):
        x = (place.x + d) % NX
        copy = remote(
            packed.at[pl.ds(x * 2, 2)], near.at[d - 1], send.at[d], recv.at[d], place.at(dx=d)
        )
        copy.start()
        pending.append(copy)
    for copy in pending:
        copy.wait_recv()

    def gathered(which):
        who = place.x * 2 + which
        parts = [unpack(packed[who])] + [unpack(near[d, which]) for d in range(NX - 1)]
        return merge(parts, who)

    total, facts, _ = gathered(1 - side)
    leaving[0:Q_COLS, :] = total.astype(BF16)
    leaving[Q_COLS:, :] = stack_rows(split_rows(facts), PACK - Q_COLS).astype(BF16)
    copy = remote(leaving, far, send.at[0], recv.at[0], place.at(dz=4))
    copy.start()
    pending.append(copy)
    total, facts, _ = gathered(side)
    copy.wait_recv()
    total, facts, in_first = merge([(total, facts), unpack(far[...])], place.owner())
    for copy in pending:
        copy.wait_send()
    return total / jnp.where(in_first, facts[2], facts[3])


MERGE_SCRATCH = [
    pltpu.VMEM((NX - 1, 2, PACK, TOKENS), BF16),
    pltpu.VMEM((PACK, TOKENS), BF16),
    pltpu.VMEM((PACK, TOKENS), BF16),
    pltpu.SemaphoreType.DMA((NX,)),
    pltpu.SemaphoreType.DMA((NX,)),
]


def exit_kernel(
    packed, stream, gain, out_w, gate_w, up_w, down_w, layer_out,
    out_buf, gate_buf, up_buf, down_buf, hidden, attended, load_sems, *comm
):
    joining, first, gather, second = comm[:5], comm[5:18], comm[18:24], comm[24:]
    place = Place()
    ready = greet(place)
    loads = [
        pltpu.make_async_copy(src, dst, load_sems.at[k])
        for k, (src, dst) in enumerate(
            (
                (out_w, out_buf.at[0:Q_COLS]),
                (gate_w, gate_buf),
                (up_w, up_buf),
                (down_w, down_buf),
            )
        )
    ]
    for load in loads:
        load.start()
    out_buf[Q_COLS:, :] = jnp.zeros((128 - Q_COLS, WIDTH), BF16)
    ready()
    columns = merge_owners(place, packed, *joining)
    columns = jnp.concatenate([columns, jnp.zeros((128 - Q_COLS, TOKENS), F32)], axis=0)
    attended[...] = columns.T.astype(BF16).reshape(attended.shape)
    loads[0].wait()

    def out_term(cls, cols):
        return jnp.dot(attended[cls], out_buf[:, cols], preferred_element_type=F32)

    summed = scatter_sums(place, out_term, first)
    mixed = (stream[...].astype(F32) + summed).astype(BF16)
    block = rms_block(mixed.astype(F32), gain)
    gather_rows(place, block, gather)
    loads[1].wait()
    loads[2].wait()

    def hide(cls):
        rows = gather[2][cls]
        gate = jnp.dot(rows, gate_buf[...], preferred_element_type=F32)
        up = jnp.dot(rows, up_buf[...], preferred_element_type=F32)
        hidden[cls] = (gate / (1.0 + jnp.exp(-gate)) * up).astype(BF16)

    hide(place.c)
    gather_pair_wait(place, gather)
    hide(1 - place.c)
    loads[3].wait()

    def down_term(cls, cols):
        return jnp.dot(hidden[cls], down_buf[:, cols], preferred_element_type=F32)

    summed = scatter_sums(place, down_term, second)
    layer_out[...] = (mixed.astype(F32) + summed).astype(BF16)


VM = pl.BlockSpec(memory_space=pltpu.VMEM)
SM = pl.BlockSpec(memory_space=pltpu.SMEM)
ANY = pl.BlockSpec(memory_space=pl.ANY)
VMEM_BYTES = 60 * 2**20


def entry(stream, gain, query_w, kv_w, query_b, kv_b, cache, mig_from):
    page = (PAGE_TOKENS, 2 * HEAD_SIZE)
    return pl.pallas_call(
        entry_kernel,
        out_shape=(
            jax.ShapeDtypeStruct((OWNERS, 2, CLASS_ROWS, 128), BF16),
            jax.ShapeDtypeStruct((MIGRATED,) + page, BF16),
        ),
        in_specs=[VM, VM, ANY, ANY, VM, VM, ANY, SM],
        out_specs=(VM, VM),
        scratch_shapes=[
            pltpu.VMEM((128, WIDTH), BF16),
            pltpu.VMEM((SLOTS,) + page, BF16),
            pltpu.VMEM((MIGRATED,) + page, BF16),
            pltpu.SemaphoreType.DMA((3,)),
            pltpu.SemaphoreType.DMA((2,)),
            pltpu.SemaphoreType.DMA((14,)),
            pltpu.SemaphoreType.DMA((14,)),
        ]
        + GATHER_SCRATCH,
        compiler_params=pltpu.CompilerParams(
            collective_id=0, has_side_effects=True, vmem_limit_bytes=VMEM_BYTES
        ),
        name="entry",
    )(stream, gain, query_w, kv_w, query_b, kv_b, cache, mig_from)


def attend(pieces, landed, cache, lengths, page_table, new_pages, mig_to):
    return pl.pallas_call(
        attend_kernel,
        out_shape=(
            jax.ShapeDtypeStruct((OWNERS, PACK, TOKENS), BF16),
            jax.ShapeDtypeStruct((1,) + cache.shape, BF16),
        ),
        in_specs=[VM, VM, VM, SM, VM, VM, SM, SM],
        out_specs=(VM, VM),
        scratch_shapes=[
            pltpu.VMEM((QUERY_PER_KV, TOKENS, HEAD_SIZE), BF16),
            pltpu.VMEM((QUERY_PER_KV * HEAD_SIZE, TOKENS), BF16),
        ],
        compiler_params=pltpu.CompilerParams(vmem_limit_bytes=VMEM_BYTES),
        name="attend",
    )(pieces, landed, cache, lengths, page_table, new_pages, new_pages, mig_to)


def leave(packed, stream, gain, out_w, gate_w, up_w, down_w):
    buffers = [
        pltpu.VMEM(shape, BF16)
        for shape in ((128, WIDTH), gate_w.shape, up_w.shape, down_w.shape)
    ]
    return pl.pallas_call(
        exit_kernel,
        out_shape=jax.ShapeDtypeStruct((ROWS, WIDTH), BF16),
        in_specs=[VM, VM, VM, ANY, ANY, ANY, ANY],
        out_specs=VM,
        scratch_shapes=buffers
        + [
            pltpu.VMEM((2, CLASS_ROWS, gate_w.shape[1]), BF16),
            pltpu.VMEM((2, CLASS_ROWS, 128), BF16),
            pltpu.SemaphoreType.DMA((4,)),
        ]
        + MERGE_SCRATCH
        + SCATTER_SCRATCH
        + GATHER_SCRATCH
        + SCATTER_SCRATCH,
        compiler_params=pltpu.CompilerParams(
            collective_id=1, has_side_effects=True, vmem_limit_bytes=VMEM_BYTES
        ),
        name="leave",
    )(packed, stream, gain, out_w, gate_w, up_w, down_w)


def per_device(
    stream,
    attn_gain,
    query_weight,
    query_bias_input,
    key_value_weight,
    key_value_bias,
    output_weight,
    mlp_gain,
    w_gate,
    w_up,
    w_down,
    paged_cache_input,
    lengths,
    page_table,
    new_pages,
    mig_from,
    mig_to,
):
    lines = (WIDTH // 128, 128)
    cache = paged_cache_input[0]
    pieces, landed = entry(
        stream,
        attn_gain.reshape(lines),
        query_weight[:, 0, :].T,
        key_value_weight[:, 0, :].T,
        query_bias_input,
        key_value_bias,
        cache,
        mig_from,
    )
    packed, updated_cache = attend(pieces, landed, cache, lengths, page_table, new_pages, mig_to)
    layer_out = leave(
        packed, stream, mlp_gain.reshape(lines), output_weight[0], w_gate, w_up, w_down
    )
    return (layer_out, updated_cache)


def solution(mesh):
    placed = (
        P(("rep", "tp"), None),
        P(),
        P(None, "tp", None),
        P("tp", None),
        P(None, "tp", None),
        P("tp", None),
        P("tp", None, None),
        P(),
        P(None, "tp"),
        P(None, "tp"),
        P("tp", None),
        P(("rep", "tp"), None, None, None),
        P("rep"),
        P("rep", None),
        P("rep", None),
        P("rep", None),
        P("rep", None),
    )
    return jax.shard_map(
        per_device,
        mesh=mesh,
        in_specs=placed,
        out_specs=(P(("rep", "tp"), None), P(("rep", "tp"), None, None, None)),
        check_vma=False,
    )
```
